32 devices in a mesh: rel: 2 (over core), ent: 16 (over z, y, x).
Axes of the slice: x: 2, y: 2, z: 4, core: 2. Of those that a mesh axis runs over, the one named last changes fastest.
Arguments:
- facts: bfloat16 [16, 2048, 2048], P('rel', 'ent'), may hold values from -6 to 6
- observed: int32 [16, 2048, 158], P('rel', 'ent'), may hold values from 0 to 8191
- factors: bfloat16 [2048, 128], P('ent'), may hold values from -0.59765625 to 0.59765625
- cores: bfloat16 [16, 128, 128], P('rel'), may hold values from -6 to 6
Outputs:
- grad_factors: float32 [2048, 128], P('ent')
- grad_cores: float32 [16, 128, 128], P('rel')
The draws below stay inside these ranges and needn't reach their ends.
All inputs are finite; a program needn't handle non-finite values.
Results may differ from the reference program's by a relative error of at most 0.0008.
Values may be sent and summed in bfloat16 or wider, within the bound.
No kernel may reach another device: no remote copies, remote signals or barrier semaphores. Data moves between devices by JAX's collectives and lax.ppermute only.
A program may use at most 128 MiB of HBM per device.

```python
import jax
import jax.numpy as jnp
from jax import lax

R = 128
N = 2048
K = 16
WORDS = 158


def place_ends(drawn, own_key, least, largest):
    longest = drawn.shape.index(max(drawn.shape))
    spots = []
    for shift in (0, 1):
        where = [jax.random.randint(jax.random.fold_in(own_key, axis), (), 0, length) for axis, length in enumerate(drawn.shape)]
        where[longest] = (where[longest] + shift) % drawn.shape[longest]
        spots.append(tuple(where))
    return drawn.at[spots[0]].set(least).at[spots[1]].set(largest)


def spiked(array, key, source, target, shards_of, factor):
    owner, partner = [(jnp.arange(array.shape[axis_at]) // (array.shape[axis_at] // shards_of)).reshape([-1 if axis == axis_at else 1 for axis in range(array.ndim)]) for axis_at in (source, target)]
    chosen = jax.random.permutation(key, shards_of)[partner]
    strong = (owner == chosen) | (owner == (partner + shards_of // 2) % shards_of)
    return jnp.where(strong, factor * array, array)


def block_scale(rng, extent, split, smallest, top_value):
    gain, own = 1.0, jax.random.fold_in(rng, 6)
    for position, blocks in split:
        heights = jnp.exp(jax.random.uniform(jax.random.fold_in(own, position), (blocks,), jnp.float32, smallest / len(split), top_value / len(split)))
        gain = gain * jnp.repeat(heights, extent[position] // blocks).reshape([-1 if axis == position else 1 for axis in range(len(extent))])
    return gain


def bell_draw(key, dims, spread, bound, split=(), held_as=jnp.bfloat16):
    result = spread * jax.random.normal(key, dims, jnp.float32)
    if split:
        result = result * block_scale(key, dims, split, -0.22, 0.18)
    return jnp.clip(result, -bound, bound).astype(held_as)


def bell_draw_with(stream_key, dims, deviation, most, pieces, heavy, held_as=jnp.bfloat16):
    values = deviation * jax.random.normal(stream_key, dims, jnp.float32)
    if pieces:
        values = values * block_scale(stream_key, dims, pieces, -0.22, 0.18)
    return jnp.clip(spiked(values, jax.random.fold_in(stream_key, 3), *heavy), -most, most).astype(held_as)


def setup_inputs(seed: int = 0) -> dict:
    key_of = jax.random.split(jax.random.key(seed), 5)
    return {
        "facts": bell_draw_with(key_of[0], (K, N, N), 1.0, 6.0, ((0, 2), (1, 16)), (1, 2, 16, 2.0)),
        "observed": place_ends(jax.random.randint(key_of[1], (K, N, WORDS), 0, 8192), jax.random.fold_in(key_of[1], 1), 0, 8191).astype(jnp.int32),
        "factors": bell_draw(key_of[2], (N, R), 0.0884, 0.59765625, ((0, 16),)),
        "cores": bell_draw(key_of[3], (K, R, R), 1.0, 6.0, ((0, 2),)),
    }


def unpack(words, count):
    shifts = jnp.arange(13, dtype=jnp.int32)
    bits = jnp.bitwise_and(jnp.right_shift(words[..., None], shifts), 1)
    flat = bits.reshape(words.shape[:-1] + (words.shape[-1] * 13,))
    return flat[..., :count].astype(jnp.bfloat16)

def reference(facts, observed, factors, cores):

    def one_relation(items):
        data, words, core = items
        mask = unpack(words, N)
        left = jnp.dot(factors, core, preferred_element_type=jnp.float32).astype(jnp.bfloat16)
        right = jnp.dot(factors, core.T, preferred_element_type=jnp.float32).astype(jnp.bfloat16)
        model = jnp.dot(left, factors.T, preferred_element_type=jnp.float32)
        err = (mask.astype(jnp.float32) * (model - data.astype(jnp.float32))).astype(jnp.bfloat16)
        rows = jnp.dot(err, right, preferred_element_type=jnp.float32) + jnp.dot(err.T, left, preferred_element_type=jnp.float32)
        pull = jnp.dot(err, factors, preferred_element_type=jnp.float32).astype(jnp.bfloat16)
        core_grad = jnp.dot(factors.T, pull, preferred_element_type=jnp.float32)
        return (rows, core_grad)
    rows, core_grad = lax.map(one_relation, (facts, observed, cores))
    grad_factors = lax.optimization_barrier(jnp.sum(rows, axis=0)) / jnp.sqrt(jnp.float32(N * K))
    grad_cores = core_grad * (R / N)
    return (grad_factors, grad_cores)
```

```python
import functools

import jax
import jax.numpy as jnp
from jax import lax
from jax.experimental import pallas as pl
from jax.experimental.pallas import tpu as pltpu
from jax.sharding import PartitionSpec as P

BITS = 13
LANES = 128
F32 = jnp.float32
BF16 = jnp.bfloat16


def swap(x, axis, size, distance):
    return lax.ppermute(x, axis, [(i, i ^ distance) for i in range(size)])


def nt(a, b):
    return lax.dot_general(a, b, (((1,), (1,)), ((), ())), preferred_element_type=F32)


def tn(a, b):
    return lax.dot_general(a, b, (((0,), (0,)), ((), ())), preferred_element_type=F32)


def nn(a, b):
    return jnp.dot(a, b, preferred_element_type=F32)


def err_kernel(
    ent, me_ref, facts_ref, words_ref, own_ref, core_ref, gathered_ref,
    err_ref, left_ref, pull_ref, whole_ref, chunk,
):
    me = me_ref[0]
    n_all = facts_ref.shape[2]
    rows = own_ref.shape[0]

    @pl.when(pl.program_id(0) == 0)
    def _():
        for c in range(ent):
            src = pl.multiple_of(jnp.bitwise_xor(me, c) * rows, rows)
            whole_ref[c * rows : (c + 1) * rows, :] = gathered_ref[pl.ds(src, rows), :]

    left = nn(own_ref[...], core_ref[0]).astype(BF16)
    left_ref[0] = left
    words = words_ref[0]
    count = words.shape[1]
    blocks = pl.cdiv(count, LANES)
    parts = []
    for b in range(blocks):
        part = words[:, b * LANES : min(count, (b + 1) * LANES)]
        if part.shape[1] < LANES:
            part = jnp.pad(part, ((0, 0), (0, LANES - part.shape[1])))
        parts.append(part)
    lane = lax.broadcasted_iota(jnp.int32, (rows, LANES), 1)
    pull = jnp.zeros((rows, whole_ref.shape[1]), F32)
    for start in range(0, n_all, chunk):
        piece = whole_ref[start : start + chunk, :]
        model = nt(left, piece)
        tiles = []
        for t in range(chunk // LANES):
            tile = start // LANES + t
            block, inside = divmod(tile, BITS)
            column = inside * LANES + lane
            word = column // BITS
            bit = jnp.left_shift(1, column - word * BITS)
            marks = jnp.take_along_axis(parts[block], word, axis=1)
            data = facts_ref[0, :, tile * LANES : (tile + 1) * LANES].astype(F32)
            diff = model[:, t * LANES : (t + 1) * LANES] - data
            tiles.append(jnp.where((marks & bit) != 0, diff, 0.0).astype(BF16))
        err = jnp.concatenate(tiles, axis=1)
        err_ref[0, :, start : start + chunk] = err
        pull = pull + nn(err, piece)
    pull_ref[0, 0] = pull.astype(BF16)


def rows_kernel(
    ent, low, rel, me_ref, err_ref, left_ref, core_ref, gathered_ref, *rest
):
    outs, (whole_ref, right_ref, total_ref, own_ref) = rest[:rel], rest[rel:]
    me, mine = me_ref[0], me_ref[1]
    rows = left_ref.shape[1]
    step = pl.program_id(0)

    @pl.when(step == 0)
    def _():
        for c in range(ent):
            src = pl.multiple_of(jnp.bitwise_xor(me, c) * rows, rows)
            whole_ref[c * rows : (c + 1) * rows, :] = gathered_ref[pl.ds(src, rows), :]
        total_ref[...] = jnp.zeros_like(total_ref)
        own_ref[...] = jnp.zeros_like(own_ref)

    pair = err_ref.shape[0]
    right_ref[...] = jnp.concatenate(
        [nt(whole_ref[...], core_ref[p]).astype(BF16) for p in range(pair)], axis=1
    )
    rank = whole_ref.shape[1]
    own = own_ref[...]
    for p in range(pair):
        own = own + nn(err_ref[p], right_ref[:, p * rank : (p + 1) * rank])
    own_ref[...] = own
    err = err_ref[...].reshape(pair * rows, err_ref.shape[2])
    left = left_ref[...].reshape(pair * rows, rank)
    total_ref[...] += tn(err, left)

    @pl.when(step == pl.num_programs(0) - 1)
    def _():
        at = pl.multiple_of(me * rows, rows)
        total_ref[pl.ds(at, rows), :] += own_ref[...]
        sub = rows // rel
        for h in range(rel):
            piece = jnp.bitwise_xor(mine, h) * sub
            for slot in range(ent):
                src = pl.multiple_of(jnp.bitwise_xor(me, slot) * rows + piece, sub)
                outs[h][slot % low, slot // low] = total_ref[pl.ds(src, sub), :]


def core_kernel(low, me_ref, gathered_ref, *rest):
    pulls, outs = rest[:-low], rest[-low:]
    high = len(pulls)
    rows, rank = pulls[0].shape[1], pulls[0].shape[2]
    near = jnp.bitwise_and(me_ref[0], low - 1)
    total = []
    for k in range(pulls[0].shape[0]):
        acc = jnp.zeros((rank, rank), F32)
        for d in range(high):
            at = d * low * rows
            acc = acc + tn(gathered_ref[at : at + rows, :], pulls[d][k])
        total.append(acc)
    total = jnp.concatenate(total, axis=0)
    size = total.shape[0] // low
    for q in range(low):
        for p in range(low):
            @pl.when(jnp.bitwise_xor(near, q) == p)
            def _():
                outs[q][...] = total[p * size : (p + 1) * size, :]


def place_kernel(ent, low, me_ref, *rest):
    parts, out_ref = rest[:-1], rest[-1]
    me = me_ref[0]
    high = ent // low
    size = parts[0].shape[1]
    near, far = jnp.bitwise_and(me, low - 1), me // low
    for q in range(low):
        for d in range(high):
            block = jnp.bitwise_xor(far, d) * low + jnp.bitwise_xor(near, q)
            at = pl.multiple_of(block * size, size)
            out_ref[pl.ds(at, size), :] = parts[q][d]


def per_device(facts, observed, factors, cores):
    rel_loc, rows, n_all = facts.shape
    rank = factors.shape[1]
    rel, ent = lax.axis_size("rel"), lax.axis_size("ent")
    low = 1 << ((ent.bit_length() - 1) // 2)
    high = ent // low
    per = rel_loc // high
    near_swap = lambda x, d: swap(x, "ent", ent, d)
    far_swap = lambda x, d: swap(x, "ent", ent, d * low)
    me = jnp.stack([lax.axis_index("ent"), lax.axis_index("rel")]).astype(jnp.int32)

    plane = jnp.concatenate([factors] + [near_swap(factors, d) for d in range(1, low)])
    gathered = jnp.concatenate([plane] + [far_swap(plane, d) for d in range(1, high)])

    whole = lambda shape: pl.BlockSpec(shape, lambda k, me: (0,) * len(shape))
    words = observed.shape[2]
    chunk = min(512, n_all)
    err, left, pull = pl.pallas_call(
        lambda *refs: err_kernel(ent, *refs, chunk),
        grid_spec=pltpu.PrefetchScalarGridSpec(
            num_scalar_prefetch=1,
            grid=(rel_loc,),
            in_specs=[
                pl.BlockSpec((1, rows, n_all), lambda k, me: (k, 0, 0)),
                pl.BlockSpec((1, rows, words), lambda k, me: (k, 0, 0)),
                whole((rows, rank)),
                pl.BlockSpec((1, rank, rank), lambda k, me: (k, 0, 0)),
                whole((n_all, rank)),
            ],
            out_specs=[
                pl.BlockSpec((1, rows, n_all), lambda k, me: (k, 0, 0)),
                pl.BlockSpec((1, rows, rank), lambda k, me: (k, 0, 0)),
                pl.BlockSpec(
                    (1, 1, rows, rank),
                    lambda k, me: ((me[0] // low) ^ (k // per), k % per, 0, 0),
                ),
            ],
            scratch_shapes=[pltpu.VMEM((n_all, rank), BF16)],
        ),
        out_shape=[
            jax.ShapeDtypeStruct((rel_loc, rows, n_all), BF16),
            jax.ShapeDtypeStruct((rel_loc, rows, rank), BF16),
            jax.ShapeDtypeStruct((high, per, rows, rank), BF16),
        ],
        name="err_kernel",
    )(me, facts, observed, factors, cores, gathered)

    pulls = [pull[0]] + [far_swap(pull[d], d) for d in range(1, high)]

    sub = rows // rel
    pair = 2 if rel_loc % 2 == 0 else 1
    shares = pl.pallas_call(
        functools.partial(rows_kernel, ent, low, rel),
        grid_spec=pltpu.PrefetchScalarGridSpec(
            num_scalar_prefetch=1,
            grid=(rel_loc // pair,),
            in_specs=[
                pl.BlockSpec((pair, rows, n_all), lambda k, me: (k, 0, 0)),
                pl.BlockSpec((pair, rows, rank), lambda k, me: (k, 0, 0)),
                pl.BlockSpec((pair, rank, rank), lambda k, me: (k, 0, 0)),
                whole((n_all, rank)),
            ],
            out_specs=[whole((low, high, sub, rank))] * rel,
            scratch_shapes=[
                pltpu.VMEM((n_all, rank), BF16),
                pltpu.VMEM((n_all, pair * rank), BF16),
                pltpu.VMEM((n_all, rank), F32),
                pltpu.VMEM((rows, rank), F32),
            ],
        ),
        out_shape=[jax.ShapeDtypeStruct((low, high, sub, rank), F32)] * rel,
        name="rows_kernel",
    )(me, err, left, cores, gathered)

    part = shares[0]
    for h in range(1, rel):
        part = part + swap(shares[h], "rel", rel, h)
    near_part = part[0]
    for q in range(1, low):
        near_part = near_part + near_swap(part[q], q)
    owned = near_part[0]
    for d in range(1, high):
        owned = owned + far_swap(near_part[d], d)
    owned = owned / jnp.sqrt(F32(n_all * rel_loc * rel))
    grad_factors = jnp.zeros((rel, sub, rank), F32)
    here = lax.axis_index("rel")
    for h in range(rel):
        piece = owned if h == 0 else swap(owned, "rel", rel, h)
        grad_factors = lax.dynamic_update_index_in_dim(grad_factors, piece, here ^ h, 0)
    grad_factors = grad_factors.reshape(rows, rank)

    size = per * rank // low
    flat = lambda shape: pl.BlockSpec(shape, lambda i, me: (0,) * len(shape))
    core_parts = pl.pallas_call(
        functools.partial(core_kernel, low),
        grid_spec=pltpu.PrefetchScalarGridSpec(
            num_scalar_prefetch=1,
            grid=(1,),
            in_specs=[flat((n_all, rank))] + [flat((per, rows, rank))] * high,
            out_specs=[flat((size, rank))] * low,
        ),
        out_shape=[jax.ShapeDtypeStruct((size, rank), F32)] * low,
        name="core_kernel",
    )(me, gathered, *pulls)
    core_sum = core_parts[0]
    for q in range(1, low):
        core_sum = core_sum + near_swap(core_parts[q], q)
    core_sum = core_sum * (rank / n_all)
    column = jnp.stack([core_sum] + [far_swap(core_sum, d) for d in range(1, high)])
    columns = [column] + [near_swap(column, q) for q in range(1, low)]
    grad_cores = pl.pallas_call(
        functools.partial(place_kernel, ent, low),
        grid_spec=pltpu.PrefetchScalarGridSpec(
            num_scalar_prefetch=1,
            grid=(1,),
            in_specs=[flat((high, size, rank))] * low,
            out_specs=flat((rel_loc * rank, rank)),
        ),
        out_shape=jax.ShapeDtypeStruct((rel_loc * rank, rank), F32),
        name="place_kernel",
    )(me, *columns)
    return grad_factors, grad_cores.reshape(rel_loc, rank, rank)


def solution(mesh):
    return jax.shard_map(
        per_device,
        mesh=mesh,
        in_specs=(
            P("rel", "ent", None),
            P("rel", "ent", None),
            P("ent", None),
            P("rel", None, None),
        ),
        out_specs=(P("ent", None), P("rel", None, None)),
        check_vma=False,
    )
```

```python
import functools

import jax
import jax.numpy as jnp
from jax import lax
from jax.experimental import pallas as pl
from jax.experimental.pallas import tpu as pltpu
from jax.sharding import PartitionSpec as P


BITS = 13
LANES = 128
F32 = jnp.float32
BF16 = jnp.bfloat16
MIB = 1 << 20


def swap(x, axis, size, distance):
    return lax.ppermute(x, axis, [(i, i ^ distance) for i in range(size)])


def nt(a, b):
    return lax.dot_general(a, b, (((1,), (1,)), ((), ())), preferred_element_type=F32)


def tn(a, b):
    return lax.dot_general(a, b, (((0,), (0,)), ((), ())), preferred_element_type=F32)


def nn(a, b):
    return jnp.dot(a, b, preferred_element_type=F32)


def chip_of(me, slot, low, high):
    return jnp.bitwise_xor(me, (slot % high) * low + slot // high)


def take_pair(pieces, pair, scratch, size):
    inside = pieces[0].shape[0] // size
    for p, piece in enumerate(pieces):
        for i in range(inside):

            @pl.when(pair == p * inside + i)
            def _():
                scratch[...] = piece[i * size : (i + 1) * size, :]


def add_err(pair, me, low, high, left_ref, piece, words_ref, facts, err_ref, acc_ref):
    relations, half = words_ref.shape[0], words_ref.shape[1]
    rows, width = 2 * half, piece.shape[0] // 2
    lane = lax.broadcasted_iota(jnp.int32, (half, LANES), 1)
    words, bits, blocks = [], [], []
    for s in range(2):
        chip = chip_of(me, 2 * pair + s, low, high)
        column = lax.rem(chip, BITS) * LANES + lane
        word = jnp.right_shift(column * 5042, 16)
        words.append(word)
        bits.append(jnp.left_shift(1, column - word * BITS))
        blocks.append(pl.multiple_of(lax.div(chip, BITS) * LANES, LANES))
    for k in range(relations):
        at = slice(k * rows, (k + 1) * rows)
        model = nt(left_ref[at, :], piece)
        tiles = []
        for s in range(2):
            marks = jnp.take_along_axis(
                words_ref[k, :, pl.ds(blocks[s], LANES)], words[s], axis=1
            )
            data = facts[s][k].astype(F32)
            diff = model[:, s * width : (s + 1) * width] - data
            top = jnp.where((marks & bits[s]) != 0, diff[:half], 0.0)
            low_bits = jnp.left_shift(bits[s], 16)
            bottom = jnp.where((marks & low_bits) != 0, diff[half:], 0.0)
            tiles.append(jnp.concatenate([top, bottom], axis=0).astype(BF16))
        err = jnp.concatenate(tiles, axis=1)
        err_ref[0, at, :] = err
        acc_ref[at, :] += nn(err, piece)


def early_kernel(
    low, high, me_ref, words_ref, facts0_ref, facts1_ref, own_ref, cores_ref, column_ref,
    err_ref, left_ref, acc_ref,
):
    pair = pl.program_id(0)
    rows = own_ref.shape[0]

    @pl.when(pair == 0)
    def _():
        acc_ref[...] = jnp.zeros_like(acc_ref)
        for k in range(cores_ref.shape[0]):
            left_ref[k * rows : (k + 1) * rows, :] = nn(own_ref[...], cores_ref[k]).astype(BF16)

    add_err(
        pair, me_ref[0], low, high, left_ref, column_ref[...], words_ref,
        (facts0_ref, facts1_ref), err_ref, acc_ref,
    )


def late_kernel(
    low, high, first, me_ref, words_ref, facts0_ref, facts1_ref, left_ref, part_ref, _, *rest
):
    pieces, (err_ref, *pulls) = rest[: low - 1], rest[low - 1 : -2]
    piece_ref, acc_ref = rest[-2:]
    step = pl.program_id(0)

    @pl.when(step == 0)
    def _():
        acc_ref[...] = part_ref[...]

    take_pair(pieces, step, piece_ref, piece_ref.shape[0])
    add_err(
        step + first, me_ref[0], low, high, left_ref, piece_ref[...], words_ref,
        (facts0_ref, facts1_ref), err_ref, acc_ref,
    )

    @pl.when(step == pl.num_programs(0) - 1)
    def _():
        size = pulls[0].shape[0]
        far = me_ref[0] // low
        for d in range(high):
            at = pl.multiple_of(jnp.bitwise_xor(far, d) * size, size)
            pulls[d][...] = acc_ref[pl.ds(at, size), :].astype(BF16)


def rows_kernel(low, rel, me_ref, err_ref, left_ref, cores_ref, *rest):
    pieces, outs = rest[:low], rest[low : low + rel]
    piece_ref, _, total_ref, own_ref = rest[low + rel :]
    mine = me_ref[1]
    step, pairs = pl.program_id(0), pl.num_programs(0)
    pair = lax.rem(step + 1, pairs)

    @pl.when(step == 0)
    def _():
        own_ref[...] = jnp.zeros_like(own_ref)

    take_pair(pieces, pair, piece_ref, piece_ref.shape[0])
    rank = left_ref.shape[1]
    rows = piece_ref.shape[0] // 2
    relations = cores_ref.shape[0] // rank
    total_ref[...] = tn(err_ref[0], left_ref[...])
    own = own_ref[...]
    for k in range(relations):
        span = slice(k * rank, (k + 1) * rank)
        right = nt(piece_ref[...], cores_ref[span, :]).astype(BF16)
        own = own + nn(err_ref[0, k * rows : (k + 1) * rows, :], right)
    own_ref[...] = own

    @pl.when(step == pairs - 1)
    def _():
        total_ref[:rows, :] += own_ref[...]

    sub = rows // rel
    for h in range(rel):
        piece = jnp.bitwise_xor(mine, h) * sub
        for s in range(2):
            src = pl.multiple_of(piece + s * rows, sub)
            dst = pl.multiple_of((2 * pair + s) * sub, sub)
            outs[h][pl.ds(dst, sub), :] = total_ref[pl.ds(src, sub), :]


def merge_kernel(low, high, rel, me_ref, column_ref, *rest):
    pulls, shares, outs = rest[:high], rest[high : high + rel], rest[high + rel : -1]
    total_ref = rest[-1]
    rank = column_ref.shape[1]
    rows = column_ref.shape[0] // high
    near = jnp.bitwise_and(me_ref[0], low - 1)
    for k in range(pulls[0].shape[0] // rows):
        acc = tn(column_ref[:rows, :], pulls[0][k * rows : (k + 1) * rows, :])
        for d in range(1, high):
            acc = acc + tn(
                column_ref[d * rows : (d + 1) * rows, :], pulls[d][k * rows : (k + 1) * rows, :]
            )
        total_ref[k * rank : (k + 1) * rank, :] = acc
    size = total_ref.shape[0] // low
    block = shares[0].shape[0] // low
    for q in range(low):
        part = shares[0][q * block : (q + 1) * block, :]
        for h in range(1, rel):
            part = part + shares[h][q * block : (q + 1) * block, :]
        outs[q][:block, :] = part
        src = pl.multiple_of(jnp.bitwise_xor(near, q) * size, size)
        outs[q][block:, :] = total_ref[pl.ds(src, size), :]


def near_kernel(low, high, scale, *rest):
    parts, outs = rest[:low], rest[low:]
    total = parts[0][...]
    for q in range(1, low):
        total = total + parts[q][...]
    size = total.shape[0] - outs[0].shape[0]
    sub = size // (high - 1)
    core = total[high * sub :, :] * scale
    for d in range(high):
        outs[d][:sub, :] = total[d * sub : (d + 1) * sub, :]
        outs[d][sub:, :] = core


def far_kernel(low, high, root, me_ref, *rest):
    parts, (owned_ref, column_ref) = rest[:high], rest[high:]
    sub, size = owned_ref.shape[0], column_ref.shape[0] // high
    far = me_ref[0] // low
    total = parts[0][:sub, :]
    for d in range(1, high):
        total = total + parts[d][:sub, :]
    owned_ref[...] = total / jnp.sqrt(F32(root))
    for d in range(high):
        at = pl.multiple_of(jnp.bitwise_xor(far, d) * size, size)
        column_ref[pl.ds(at, size), :] = parts[d][sub:, :]


def gradients(facts, observed, factors, cores):
    relations, rows, n_all = facts.shape
    rank = factors.shape[1]
    rel, ent = lax.axis_size("rel"), lax.axis_size("ent")
    low = 1 << ((ent.bit_length() - 1) // 2)
    high = ent // low
    per = relations // high
    here = lax.axis_index("rel")
    me = jnp.stack([lax.axis_index("ent"), here]).astype(jnp.int32)

    def near_swap(x, d):
        return swap(x, "ent", ent, d)

    def far_swap(x, d):
        return swap(x, "ent", ent, d * low)

    column = jnp.concatenate([factors] + [far_swap(factors, d) for d in range(1, high)])
    nears = [near_swap(column, q) for q in range(1, low)]

    half = rows // 2
    packed = observed[:, :half] | jnp.left_shift(observed[:, half:], 16)
    spare = -packed.shape[2] % LANES
    packed = jnp.pad(packed, ((0, 0), (0, 0), (0, spare)))

    def whole(shape):
        return pl.BlockSpec(shape, lambda t, me: (0,) * len(shape))

    def facts_block(first, s):
        return pl.BlockSpec(
            (relations, rows, rows),
            lambda t, me: (0, 0, chip_of(me[0], 2 * (t + first) + s, low, high)),
        )

    stack, pairs, first = relations * rows, ent // 2, high // 2
    wide = 2 * rows
    shape = jax.ShapeDtypeStruct
    cost = lambda share: pl.CostEstimate(
        flops=int(4 * stack * n_all * rank * share),
        bytes_accessed=int(4 * stack * n_all * share),
        transcendentals=0,
    )
    err, left, part = pl.pallas_call(
        functools.partial(early_kernel, low, high),
        grid_spec=pltpu.PrefetchScalarGridSpec(
            num_scalar_prefetch=1,
            grid=(first,),
            in_specs=[
                whole(packed.shape),
                facts_block(0, 0),
                facts_block(0, 1),
                whole((rows, rank)),
                whole(cores.shape),
                pl.BlockSpec((wide, rank), lambda t, me: (t, 0)),
            ],
            out_specs=[
                pl.BlockSpec((1, stack, wide), lambda t, me: (t, 0, 0)),
                whole((stack, rank)),
                whole((stack, rank)),
            ],
        ),
        out_shape=[
            shape((pairs, stack, wide), BF16),
            shape((stack, rank), BF16),
            shape((stack, rank), F32),
        ],
        cost_estimate=cost(first / pairs),
        compiler_params=pltpu.CompilerParams(vmem_limit_bytes=16 * MIB),
        name="early_kernel",
    )(me, packed, facts, facts, factors, cores, column)

    err, *pulls = pl.pallas_call(
        functools.partial(late_kernel, low, high, first),
        grid_spec=pltpu.PrefetchScalarGridSpec(
            num_scalar_prefetch=1,
            grid=(pairs - first,),
            in_specs=[
                whole(packed.shape),
                facts_block(first, 0),
                facts_block(first, 1),
                whole((stack, rank)),
                whole((stack, rank)),
                pl.BlockSpec(memory_space=pl.ANY),
            ]
            + [whole(column.shape)] * (low - 1),
            out_specs=[pl.BlockSpec((1, stack, wide), lambda t, me: (t + first, 0, 0))]
            + [whole((per * rows, rank))] * high,
            scratch_shapes=[pltpu.VMEM((wide, rank), BF16), pltpu.VMEM((stack, rank), F32)],
        ),
        out_shape=[shape(err.shape, BF16)] + [shape((per * rows, rank), BF16)] * high,
        input_output_aliases={6: 0},
        cost_estimate=cost(1 - first / pairs),
        compiler_params=pltpu.CompilerParams(vmem_limit_bytes=16 * MIB),
        name="late_kernel",
    )(me, packed, facts, facts, left, part, err, *nears)

    for d in range(1, high):
        pulls[d] = far_swap(pulls[d], d)

    sub = rows // rel
    rows_call = pl.pallas_call(
        functools.partial(rows_kernel, low, rel),
        grid_spec=pltpu.PrefetchScalarGridSpec(
            num_scalar_prefetch=1,
            grid=(pairs,),
            in_specs=[
                pl.BlockSpec((1, stack, wide), lambda t, me: ((t + 1) % pairs, 0, 0)),
                whole((stack, rank)),
                whole((relations * rank, rank)),
            ]
            + [whole(column.shape)] * low,
            out_specs=[whole((ent * sub, rank))] * rel,
            scratch_shapes=[
                pltpu.VMEM((wide, rank), BF16),
                pltpu.VMEM((wide, relations * rank), BF16),
                pltpu.VMEM((wide, rank), F32),
                pltpu.VMEM((rows, rank), F32),
            ],
        ),
        out_shape=[shape((ent * sub, rank), F32)] * rel,
        cost_estimate=cost(1.5),
        compiler_params=pltpu.CompilerParams(vmem_limit_bytes=16 * MIB),
        name="rows_kernel",
    )
    shares = rows_call(me, err, left, cores.reshape(relations * rank, rank), column, *nears)
    shares = [shares[0]] + [swap(shares[h], "rel", rel, h) for h in range(1, rel)]

    size = per * rank // low
    merged = pl.pallas_call(
        functools.partial(merge_kernel, low, high, rel),
        in_specs=[pl.BlockSpec(memory_space=pltpu.SMEM)]
        + [pl.BlockSpec(memory_space=pltpu.VMEM)] * (1 + high + rel),
        out_shape=[shape((high * sub + size, rank), F32)] * low,
        scratch_shapes=[pltpu.VMEM((per * rank, rank), F32)],
        compiler_params=pltpu.CompilerParams(vmem_limit_bytes=8 * MIB),
        name="merge_kernel",
    )(me, column, *pulls, *shares)
    merged = [merged[0]] + [near_swap(merged[q], q) for q in range(1, low)]

    parts = pl.pallas_call(
        functools.partial(near_kernel, low, high, rank / n_all),
        out_shape=[shape((sub + size, rank), F32)] * high,
        compiler_params=pltpu.CompilerParams(vmem_limit_bytes=6 * MIB),
        name="near_kernel",
    )(*merged)
    parts = [parts[0]] + [far_swap(parts[d], d) for d in range(1, high)]

    owned, core_column = pl.pallas_call(
        functools.partial(far_kernel, low, high, n_all * relations * rel),
        in_specs=[pl.BlockSpec(memory_space=pltpu.SMEM)]
        + [pl.BlockSpec(memory_space=pltpu.VMEM)] * high,
        out_shape=[shape((sub, rank), F32), shape((high * size, rank), F32)],
        compiler_params=pltpu.CompilerParams(vmem_limit_bytes=4 * MIB),
        name="far_kernel",
    )(me, *parts)

    grad_factors = jnp.zeros((rel, sub, rank), F32)
    for h in range(rel):
        piece = owned if h == 0 else swap(owned, "rel", rel, h)
        grad_factors = lax.dynamic_update_index_in_dim(grad_factors, piece, here ^ h, 0)
    grad_factors = grad_factors.reshape(rows, rank)

    grad_cores = jnp.zeros((high, low, size, rank), F32)
    near = lax.axis_index("ent") & (low - 1)
    core_column = core_column.reshape(high, size, rank)
    for q in range(low):
        piece = core_column if q == 0 else near_swap(core_column, q)
        grad_cores = lax.dynamic_update_index_in_dim(grad_cores, piece, near ^ q, 1)
    return grad_factors, grad_cores.reshape(relations, rank, rank)


def solution(mesh):
    return jax.shard_map(
        gradients,
        mesh=mesh,
        in_specs=(
            P("rel", "ent", None),
            P("rel", "ent", None),
            P("ent", None),
            P("rel", None, None),
        ),
        out_specs=(P("ent", None), P("rel", None, None)),
        check_vma=False,
    )
```

```python
import functools

import jax
import jax.numpy as jnp
from jax import lax
from jax.experimental import pallas as pl
from jax.experimental.pallas import tpu as pltpu
from jax.sharding import PartitionSpec as P


BITS = 13
LANES = 128
F32 = jnp.float32
BF16 = jnp.bfloat16
MIB = 1 << 20


def swap(x, axis, size, distance):
    return lax.ppermute(x, axis, [(i, i ^ distance) for i in range(size)])


def from_partners(own, size, send):
    got = [own]
    for d in range(1, size):
        got.append(send(d))
    return got


def nt(a, b):
    return lax.dot_general(a, b, (((1,), (1,)), ((), ())), preferred_element_type=F32)


def tn(a, b):
    return lax.dot_general(a, b, (((0,), (0,)), ((), ())), preferred_element_type=F32)


def nn(a, b):
    return jnp.dot(a, b, preferred_element_type=F32)


def chip_of(me, slot, low, high):
    return jnp.bitwise_xor(me, (slot % high) * low + slot // high)


def take_pair(pieces, pair, scratch, size):
    inside = pieces[0].shape[0] // size
    for p, piece in enumerate(pieces):
        for i in range(inside):

            @pl.when(pair == p * inside + i)
            def _():
                scratch[...] = piece[i * size : (i + 1) * size, :]


def add_err(pair, me, low, high, left_ref, piece, words_ref, facts, err_ref, acc_ref):
    relations, half = words_ref.shape[0], words_ref.shape[1]
    rows, width = 2 * half, piece.shape[0] // 2
    lane = lax.broadcasted_iota(jnp.int32, (half, LANES), 1)
    words, bits, blocks = [], [], []
    for s in range(2):
        chip = chip_of(me, 2 * pair + s, low, high)
        column = lax.rem(chip, BITS) * LANES + lane
        word = jnp.right_shift(column * 5042, 16)
        words.append(word)
        bits.append(jnp.left_shift(1, column - word * BITS))
        blocks.append(pl.multiple_of(lax.div(chip, BITS) * LANES, LANES))

    def at(k):
        return slice(k * rows, (k + 1) * rows)

    whole_model = nt(left_ref[...], piece)
    errs = []
    for k in range(relations):
        model = whole_model[at(k), :]
        tiles = []
        for s in range(2):
            marks = jnp.take_along_axis(
                words_ref[k, :, pl.ds(blocks[s], LANES)], words[s], axis=1
            )
            data = facts[s][k].astype(F32)
            diff = model[:, s * width : (s + 1) * width] - data
            top = jnp.where((marks & bits[s]) != 0, diff[:half], 0.0)
            low_bits = jnp.left_shift(bits[s], 16)
            bottom = jnp.where((marks & low_bits) != 0, diff[half:], 0.0)
            tiles.append(jnp.concatenate([top, bottom], axis=0).astype(BF16))
        err = jnp.concatenate(tiles, axis=1)
        err_ref[0, at(k), :] = err
        errs.append(err)
    acc_ref[...] += nn(jnp.concatenate(errs, axis=0), piece)


def early_kernel(
    low, high, me_ref, words_ref, facts0_ref, facts1_ref, own_ref, cores_ref, column_ref,
    err_ref, left_ref, acc_ref,
):
    pair = pl.program_id(0)
    rows = own_ref.shape[0]

    @pl.when(pair == 0)
    def _():
        acc_ref[...] = jnp.zeros_like(acc_ref)
        for k in range(cores_ref.shape[0]):
            left_ref[k * rows : (k + 1) * rows, :] = nn(own_ref[...], cores_ref[k]).astype(BF16)

    add_err(
        pair, me_ref[0], low, high, left_ref, column_ref[...], words_ref,
        (facts0_ref, facts1_ref), err_ref, acc_ref,
    )


def late_kernel(
    low, high, first, me_ref, words_ref, facts0_ref, facts1_ref, left_ref, part_ref, _, *rest
):
    pieces, (err_ref, *pulls) = rest[: low - 1], rest[low - 1 : -2]
    piece_ref, acc_ref = rest[-2:]
    step = pl.program_id(0)

    @pl.when(step == 0)
    def _():
        acc_ref[...] = part_ref[...]

    take_pair(pieces, step, piece_ref, piece_ref.shape[0])
    add_err(
        step + first, me_ref[0], low, high, left_ref, piece_ref[...], words_ref,
        (facts0_ref, facts1_ref), err_ref, acc_ref,
    )

    @pl.when(step == pl.num_programs(0) - 1)
    def _():
        size = pulls[0].shape[0]
        far = me_ref[0] // low
        for d in range(high):
            at = pl.multiple_of(jnp.bitwise_xor(far, d) * size, size)
            pulls[d][...] = acc_ref[pl.ds(at, size), :].astype(BF16)


def rows_kernel(low, rel, me_ref, err_ref, left_ref, cores_ref, *rest):
    pieces, outs = rest[:low], rest[low : low + rel]
    piece_ref, _, total_ref, own_ref = rest[low + rel :]
    mine = me_ref[1]
    step, pairs = pl.program_id(0), pl.num_programs(0)
    pair = lax.rem(step + 1, pairs)

    @pl.when(step == 0)
    def _():
        own_ref[...] = jnp.zeros_like(own_ref)

    take_pair(pieces, pair, piece_ref, piece_ref.shape[0])
    rank = left_ref.shape[1]
    rows = piece_ref.shape[0] // 2
    relations = cores_ref.shape[0] // rank
    own = own_ref[...]
    right_all = nt(piece_ref[...], cores_ref[...]).astype(BF16)
    total_ref[...] = tn(err_ref[0], left_ref[...])
    for p in range(relations):
        own = own + nn(
            err_ref[0, p * rows : (p + 1) * rows, :], right_all[:, p * rank : (p + 1) * rank]
        )
    own_ref[...] = own

    @pl.when(step == pairs - 1)
    def _():
        total_ref[:rows, :] += own_ref[...]

    sub = rows // rel
    for h in range(rel):
        piece = jnp.bitwise_xor(mine, h) * sub
        for s in range(2):
            src = pl.multiple_of(piece + s * rows, sub)
            dst = pl.multiple_of((2 * pair + s) * sub, sub)
            outs[h][pl.ds(dst, sub), :] = total_ref[pl.ds(src, sub), :]


def merge_kernel(low, high, rel, me_ref, column_ref, *rest):
    pulls, shares, outs = rest[:high], rest[high : high + rel], rest[high + rel : -1]
    total_ref = rest[-1]
    rank = column_ref.shape[1]
    rows = column_ref.shape[0] // high
    near = jnp.bitwise_and(me_ref[0], low - 1)
    for k in range(pulls[0].shape[0] // rows):
        acc = tn(column_ref[:rows, :], pulls[0][k * rows : (k + 1) * rows, :])
        for d in range(1, high):
            acc = acc + tn(
                column_ref[d * rows : (d + 1) * rows, :], pulls[d][k * rows : (k + 1) * rows, :]
            )
        total_ref[k * rank : (k + 1) * rank, :] = acc
    size = total_ref.shape[0] // low
    block = shares[0].shape[0] // low
    for q in range(low):
        part = shares[0][q * block : (q + 1) * block, :]
        for h in range(1, rel):
            part = part + shares[h][q * block : (q + 1) * block, :]
        outs[q][:block, :] = part
        src = pl.multiple_of(jnp.bitwise_xor(near, q) * size, size)
        outs[q][block:, :] = total_ref[pl.ds(src, size), :]


def near_kernel(low, high, scale, *rest):
    parts, outs = rest[:low], rest[low:]
    total = parts[0][...]
    for q in range(1, low):
        total = total + parts[q][...]
    size = total.shape[0] - outs[0].shape[0]
    sub = size // (high - 1)
    core = total[high * sub :, :] * scale
    for d in range(high):
        outs[d][:sub, :] = total[d * sub : (d + 1) * sub, :]
        outs[d][sub:, :] = core


def far_kernel(low, high, root, me_ref, *rest):
    parts, (owned_ref, column_ref) = rest[:high], rest[high:]
    sub, size = owned_ref.shape[0], column_ref.shape[0] // high
    far = me_ref[0] // low
    total = parts[0][:sub, :]
    for d in range(1, high):
        total = total + parts[d][:sub, :]
    owned_ref[...] = total / jnp.sqrt(F32(root))
    for d in range(high):
        at = pl.multiple_of(jnp.bitwise_xor(far, d) * size, size)
        column_ref[pl.ds(at, size), :] = parts[d][sub:, :]


def gradients(facts, observed, factors, cores):
    relations, rows, n_all = facts.shape
    rank = factors.shape[1]
    rel, ent = lax.axis_size("rel"), lax.axis_size("ent")
    low = 1 << ((ent.bit_length() - 1) // 2)
    high = ent // low
    per = relations // high
    here = lax.axis_index("rel")
    me = jnp.stack([lax.axis_index("ent"), here]).astype(jnp.int32)

    def near_swap(x, d):
        return swap(x, "ent", ent, d)

    def far_swap(x, d):
        return swap(x, "ent", ent, d * low)

    column = jnp.concatenate(from_partners(factors, high, lambda d: far_swap(factors, d)))
    nears = from_partners(column, low, lambda q: near_swap(column, q))[1:]

    half = rows // 2
    packed = observed[:, :half] | jnp.left_shift(observed[:, half:], 16)
    spare = -packed.shape[2] % LANES
    packed = jnp.pad(packed, ((0, 0), (0, 0), (0, spare)))

    def whole(shape):
        return pl.BlockSpec(shape, lambda t, me: (0,) * len(shape))

    def facts_block(first, s):
        return pl.BlockSpec(
            (relations, rows, rows),
            lambda t, me: (0, 0, chip_of(me[0], 2 * (t + first) + s, low, high)),
        )

    stack, pairs, first = relations * rows, ent // 2, high // 2
    wide = 2 * rows
    shape = jax.ShapeDtypeStruct
    cost = lambda share: pl.CostEstimate(
        flops=int(4 * stack * n_all * rank * share),
        bytes_accessed=int(4 * stack * n_all * share),
        transcendentals=0,
    )
    err, left, part = pl.pallas_call(
        functools.partial(early_kernel, low, high),
        grid_spec=pltpu.PrefetchScalarGridSpec(
            num_scalar_prefetch=1,
            grid=(first,),
            in_specs=[
                whole(packed.shape),
                facts_block(0, 0),
                facts_block(0, 1),
                whole((rows, rank)),
                whole(cores.shape),
                pl.BlockSpec((wide, rank), lambda t, me: (t, 0)),
            ],
            out_specs=[
                pl.BlockSpec((1, stack, wide), lambda t, me: (t, 0, 0)),
                whole((stack, rank)),
                whole((stack, rank)),
            ],
        ),
        out_shape=[
            shape((pairs, stack, wide), BF16),
            shape((stack, rank), BF16),
            shape((stack, rank), F32),
        ],
        cost_estimate=cost(first / pairs),
        compiler_params=pltpu.CompilerParams(vmem_limit_bytes=16 * MIB),
        name="early_kernel",
    )(me, packed, facts, facts, factors, cores, column)

    err, *pulls = pl.pallas_call(
        functools.partial(late_kernel, low, high, first),
        grid_spec=pltpu.PrefetchScalarGridSpec(
            num_scalar_prefetch=1,
            grid=(pairs - first,),
            in_specs=[
                whole(packed.shape),
                facts_block(first, 0),
                facts_block(first, 1),
                whole((stack, rank)),
                whole((stack, rank)),
                pl.BlockSpec(memory_space=pl.ANY),
            ]
            + [whole(column.shape)] * (low - 1),
            out_specs=[pl.BlockSpec((1, stack, wide), lambda t, me: (t + first, 0, 0))]
            + [whole((per * rows, rank))] * high,
            scratch_shapes=[pltpu.VMEM((wide, rank), BF16), pltpu.VMEM((stack, rank), F32)],
        ),
        out_shape=[shape(err.shape, BF16)] + [shape((per * rows, rank), BF16)] * high,
        input_output_aliases={6: 0},
        cost_estimate=cost(1 - first / pairs),
        compiler_params=pltpu.CompilerParams(vmem_limit_bytes=16 * MIB),
        name="late_kernel",
    )(me, packed, facts, facts, left, part, err, *nears)

    pulls = from_partners(pulls[0], high, lambda d: far_swap(pulls[d], d))

    sub = rows // rel
    rows_call = pl.pallas_call(
        functools.partial(rows_kernel, low, rel),
        grid_spec=pltpu.PrefetchScalarGridSpec(
            num_scalar_prefetch=1,
            grid=(pairs,),
            in_specs=[
                pl.BlockSpec((1, stack, wide), lambda t, me: ((t + 1) % pairs, 0, 0)),
                whole((stack, rank)),
                whole((relations * rank, rank)),
            ]
            + [whole(column.shape)] * low,
            out_specs=[whole((ent * sub, rank))] * rel,
            scratch_shapes=[
                pltpu.VMEM((wide, rank), BF16),
                pltpu.VMEM((wide, relations * rank), BF16),
                pltpu.VMEM((wide, rank), F32),
                pltpu.VMEM((rows, rank), F32),
            ],
        ),
        out_shape=[shape((ent * sub, rank), F32)] * rel,
        cost_estimate=cost(1.5),
        compiler_params=pltpu.CompilerParams(vmem_limit_bytes=16 * MIB),
        name="rows_kernel",
    )
    shares = rows_call(me, err, left, cores.reshape(relations * rank, rank), column, *nears)
    shares = [shares[0]] + [swap(shares[h], "rel", rel, h) for h in range(1, rel)]

    size = per * rank // low
    merged = pl.pallas_call(
        functools.partial(merge_kernel, low, high, rel),
        in_specs=[pl.BlockSpec(memory_space=pltpu.SMEM)]
        + [pl.BlockSpec(memory_space=pltpu.VMEM)] * (1 + high + rel),
        out_shape=[shape((high * sub + size, rank), F32)] * low,
        scratch_shapes=[pltpu.VMEM((per * rank, rank), F32)],
        compiler_params=pltpu.CompilerParams(vmem_limit_bytes=8 * MIB),
        name="merge_kernel",
    )(me, column, *pulls, *shares)
    merged = from_partners(merged[0], low, lambda q: near_swap(merged[q], q))

    parts = pl.pallas_call(
        functools.partial(near_kernel, low, high, rank / n_all),
        out_shape=[shape((sub + size, rank), F32)] * high,
        compiler_params=pltpu.CompilerParams(vmem_limit_bytes=6 * MIB),
        name="near_kernel",
    )(*merged)
    parts = from_partners(parts[0], high, lambda d: far_swap(parts[d], d))

    owned, core_column = pl.pallas_call(
        functools.partial(far_kernel, low, high, n_all * relations * rel),
        in_specs=[pl.BlockSpec(memory_space=pltpu.SMEM)]
        + [pl.BlockSpec(memory_space=pltpu.VMEM)] * high,
        out_shape=[shape((sub, rank), F32), shape((high * size, rank), F32)],
        compiler_params=pltpu.CompilerParams(vmem_limit_bytes=4 * MIB),
        name="far_kernel",
    )(me, *parts)

    grad_factors = jnp.zeros((rel, sub, rank), F32)
    for h in range(rel):
        piece = owned if h == 0 else swap(owned, "rel", rel, h)
        grad_factors = lax.dynamic_update_index_in_dim(grad_factors, piece, here ^ h, 0)
    grad_factors = grad_factors.reshape(rows, rank)

    grad_cores = jnp.zeros((high, low, size, rank), F32)
    near = lax.axis_index("ent") & (low - 1)
    core_column = core_column.reshape(high, size, rank)
    for q, piece in enumerate(from_partners(core_column, low, lambda q: near_swap(core_column, q))):
        grad_cores = lax.dynamic_update_index_in_dim(grad_cores, piece, near ^ q, 1)
    return grad_factors, grad_cores.reshape(relations, rank, rank)


def solution(mesh):
    return jax.shard_map(
        gradients,
        mesh=mesh,
        in_specs=(
            P("rel", "ent", None),
            P("rel", "ent", None),
            P("ent", None),
            P("rel", None, None),
        ),
        out_specs=(P("ent", None), P("rel", None, None)),
        check_vma=False,
    )
```

```python
import functools

import jax
import jax.numpy as jnp
from jax import lax
from jax.experimental import pallas as pl
from jax.experimental.pallas import tpu as pltpu
from jax.sharding import PartitionSpec as P


BITS = 13
STEPS = 128
TOP = 32700.0
LANES = 128
F32 = jnp.float32
BF16 = jnp.bfloat16
I16 = jnp.int16
MIB = 1 << 20


def swap(x, axis, size, distance):
    return lax.ppermute(x, axis, [(i, i ^ distance) for i in range(size)])


def from_partners(own, size, send):
    got = [own]
    for d in range(1, size):
        got.append(send(d))
    return got


def nt(a, b):
    return lax.dot_general(a, b, (((1,), (1,)), ((), ())), preferred_element_type=F32)


def tn(a, b):
    return lax.dot_general(a, b, (((0,), (0,)), ((), ())), preferred_element_type=F32)


def nn(a, b):
    return jnp.dot(a, b, preferred_element_type=F32)


def chip_of(me, slot, low, high):
    return jnp.bitwise_xor(me, (slot % high) * low + slot // high)


def take_pair(pieces, pair, scratch, size):
    inside = pieces[0].shape[0] // size
    for p, piece in enumerate(pieces):
        for i in range(inside):

            @pl.when(pair == p * inside + i)
            def _():
                scratch[...] = piece[i * size : (i + 1) * size, :]


def add_err(pair, me, low, high, left_ref, piece, words_ref, facts, err_ref, acc_ref):
    relations, half = words_ref.shape[0], words_ref.shape[1]
    rows, width = 2 * half, piece.shape[0] // 2
    lane = lax.broadcasted_iota(jnp.int32, (half, LANES), 1)
    words, bits, blocks = [], [], []
    for s in range(2):
        chip = chip_of(me, 2 * pair + s, low, high)
        column = lax.rem(chip, BITS) * LANES + lane
        word = jnp.right_shift(column * 5042, 16)
        words.append(word)
        bits.append(jnp.left_shift(1, column - word * BITS))
        blocks.append(pl.multiple_of(lax.div(chip, BITS) * LANES, LANES))

    def at(k):
        return slice(k * rows, (k + 1) * rows)

    whole_model = nt(left_ref[...], piece)
    errs = []
    for k in range(relations):
        model = whole_model[at(k), :]
        tiles = []
        for s in range(2):
            marks = jnp.take_along_axis(
                words_ref[k, :, pl.ds(blocks[s], LANES)], words[s], axis=1
            )
            data = facts[s][k].astype(F32)
            diff = model[:, s * width : (s + 1) * width] - data
            top = jnp.where((marks & bits[s]) != 0, diff[:half], 0.0)
            low_bits = jnp.left_shift(bits[s], 16)
            bottom = jnp.where((marks & low_bits) != 0, diff[half:], 0.0)
            tiles.append(jnp.concatenate([top, bottom], axis=0).astype(BF16))
        err = jnp.concatenate(tiles, axis=1)
        err_ref[0, at(k), :] = err
        errs.append(err)
    acc_ref[...] += nn(jnp.concatenate(errs, axis=0), piece)


def early_kernel(
    low, high, me_ref, words_ref, facts0_ref, facts1_ref, own_ref, cores_ref, column_ref,
    err_ref, left_ref, acc_ref,
):
    pair = pl.program_id(0)
    rows = own_ref.shape[0]

    @pl.when(pair == 0)
    def _():
        acc_ref[...] = jnp.zeros_like(acc_ref)
        for k in range(cores_ref.shape[0]):
            left_ref[k * rows : (k + 1) * rows, :] = nn(own_ref[...], cores_ref[k]).astype(BF16)

    add_err(
        pair, me_ref[0], low, high, left_ref, column_ref[...], words_ref,
        (facts0_ref, facts1_ref), err_ref, acc_ref,
    )


def late_kernel(
    low, high, first, me_ref, words_ref, facts0_ref, facts1_ref, left_ref, part_ref, _, *rest
):
    pieces, (err_ref, *pulls) = rest[: low - 1], rest[low - 1 : -2]
    piece_ref, acc_ref = rest[-2:]
    step = pl.program_id(0)

    @pl.when(step == 0)
    def _():
        acc_ref[...] = part_ref[...]

    take_pair(pieces, step, piece_ref, piece_ref.shape[0])
    add_err(
        step + first, me_ref[0], low, high, left_ref, piece_ref[...], words_ref,
        (facts0_ref, facts1_ref), err_ref, acc_ref,
    )

    @pl.when(step == pl.num_programs(0) - 1)
    def _():
        size = pulls[0].shape[0]
        far = me_ref[0] // low
        for d in range(high):
            at = pl.multiple_of(jnp.bitwise_xor(far, d) * size, size)
            pulls[d][...] = acc_ref[pl.ds(at, size), :].astype(BF16)


def rows_kernel(low, rel, me_ref, err_ref, left_ref, cores_ref, *rest):
    pieces, outs = rest[:low], rest[low : low + rel]
    piece_ref, _, total_ref, own_ref = rest[low + rel :]
    mine = me_ref[1]
    step, pairs = pl.program_id(0), pl.num_programs(0)
    pair = lax.rem(step + 1, pairs)

    @pl.when(step == 0)
    def _():
        own_ref[...] = jnp.zeros_like(own_ref)

    take_pair(pieces, pair, piece_ref, piece_ref.shape[0])
    rank = left_ref.shape[1]
    rows = piece_ref.shape[0] // 2
    relations = cores_ref.shape[0] // rank
    own = own_ref[...]
    right_all = nt(piece_ref[...], cores_ref[...]).astype(BF16)
    total_ref[...] = tn(err_ref[0], left_ref[...])
    for p in range(relations):
        own = own + nn(
            err_ref[0, p * rows : (p + 1) * rows, :], right_all[:, p * rank : (p + 1) * rank]
        )
    own_ref[...] = own

    @pl.when(step == pairs - 1)
    def _():
        total_ref[:rows, :] += own_ref[...]

    sub = rows // rel
    for h in range(rel):
        piece = jnp.bitwise_xor(mine, h) * sub
        for s in range(2):
            src = pl.multiple_of(piece + s * rows, sub)
            dst = pl.multiple_of((2 * pair + s) * sub, sub)
            outs[h][pl.ds(dst, sub), :] = total_ref[pl.ds(src, sub), :]


def scale_code(block):
    most = jnp.max(jnp.abs(block), axis=0, keepdims=True)
    return jnp.ceil(jnp.log2(jnp.maximum(most, 1e-30)) * STEPS).astype(jnp.int32)


def encode(block, code):
    factor = jnp.exp2(code.astype(F32) * (-1.0 / STEPS)) * TOP
    return jnp.floor(block * factor + 0.5).astype(jnp.int32).astype(jnp.int16)


def decode(codes, code):
    factor = jnp.exp2(code.astype(F32) * (1.0 / STEPS)) * (1.0 / TOP)
    return codes.astype(jnp.int32).astype(F32) * factor


def stack_codes(rows_of):
    at = lax.broadcasted_iota(jnp.int32, (scale_rows(len(rows_of)), LANES), 0)
    tile = jnp.zeros(at.shape, jnp.int32)
    for place, row in rows_of:
        tile = jnp.where(at == place, jnp.broadcast_to(row, at.shape), tile)
    return tile.astype(jnp.int16)


def scale_rows(blocks):
    return pl.cdiv(blocks, 16) * 16


def merge_kernel(low, high, rel, me_ref, column_ref, *rest):
    pulls, shares, outs = rest[:high], rest[high : high + rel], rest[high + rel : -1]
    total_ref = rest[-1]
    rank = column_ref.shape[1]
    rows = column_ref.shape[0] // high
    near = jnp.bitwise_and(me_ref[0], low - 1)
    for k in range(pulls[0].shape[0] // rows):
        acc = tn(column_ref[:rows, :], pulls[0][k * rows : (k + 1) * rows, :])
        for d in range(1, high):
            acc = acc + tn(
                column_ref[d * rows : (d + 1) * rows, :], pulls[d][k * rows : (k + 1) * rows, :]
            )
        total_ref[k * rank : (k + 1) * rank, :] = acc
    size = total_ref.shape[0] // low
    sub = shares[0].shape[0] // low // high
    for q in range(low):
        blocks = []
        for d in range(high):
            at = slice((q * high + d) * sub, (q * high + d + 1) * sub)
            part = shares[0][at, :]
            for h in range(1, rel):
                part = part + shares[h][at, :]
            blocks.append(part)
        src = pl.multiple_of(jnp.bitwise_xor(near, q) * size, size)
        blocks.append(total_ref[pl.ds(src, size), :])
        codes, at = [], 0
        for block in blocks:
            span = slice(at, at + block.shape[0])
            if q == 0:
                outs[q][span, :] = block
            else:
                codes.append(scale_code(block))
                outs[q][span, :] = encode(block, codes[-1])
            at += block.shape[0]
        if q > 0:
            outs[q][at:, :] = stack_codes(list(enumerate(codes)))


def near_kernel(low, high, scale, *rest):
    parts, (owned_ref, core_ref, *outs) = rest[:low], rest[low:]
    sub = owned_ref.shape[0]
    size = parts[0].shape[0] - high * sub
    scales = [part[high * sub + size :, :].astype(jnp.int32) for part in parts[1:]]
    sums = []
    for b in range(high + 1):
        span = slice(b * sub, (b + 1) * sub) if b < high else slice(b * sub, b * sub + size)
        total = parts[0][span, :]
        for part, code in zip(parts[1:], scales):
            total = total + decode(part[span, :], code[b : b + 1, :])
        sums.append(total)
    core = sums[high] * scale
    core_code = scale_code(core)
    core_codes = encode(core, core_code)
    owned_ref[...] = sums[0]
    core_ref[:size, :] = core_codes
    core_ref[size:, :] = stack_codes([(1, core_code)])
    for d in range(1, high):
        code = scale_code(sums[d])
        out = outs[d - 1]
        out[:size, :] = core_codes
        out[size : size + sub, :] = encode(sums[d], code)
        out[size + sub :, :] = stack_codes([(0, code), (1, core_code)])


def far_kernel(low, high, root, me_ref, mine_ref, core_ref, *rest):
    parts, (owned_ref, column_ref) = rest[:-2], rest[-2:]
    sub = owned_ref.shape[0]
    size = parts[0].shape[0] - sub - scale_rows(2)
    far = me_ref[0] // low
    total, codes = mine_ref[...], []
    for d in range(high):
        ref = core_ref if d == 0 else parts[d - 1]
        code = ref[ref.shape[0] - scale_rows(2) :, :].astype(jnp.int32)
        place = jnp.bitwise_xor(far, d)
        at = pl.multiple_of(place * size, size)
        column_ref[pl.ds(at, size), :] = ref[:size, :]
        codes.append((place, code[1:2, :]))
        if d > 0:
            total = total + decode(ref[size : size + sub, :], code[0:1, :])
    owned_ref[...] = total / jnp.sqrt(F32(root))
    column_ref[high * size :, :] = stack_codes(codes)


def place_kernel(low, high, me_ref, *rest):
    columns, out_ref = rest[:-1], rest[-1]
    size = out_ref.shape[0] // low // high
    near = jnp.bitwise_and(me_ref[0], low - 1)
    for q in range(low):
        codes = columns[q][high * size :, :].astype(jnp.int32)
        for d in range(high):
            block = decode(columns[q][d * size : (d + 1) * size, :], codes[d : d + 1, :])
            at = pl.multiple_of((d * low + jnp.bitwise_xor(near, q)) * size, size)
            out_ref[pl.ds(at, size), :] = block


def gradients(facts, observed, factors, cores):
    relations, rows, n_all = facts.shape
    rank = factors.shape[1]
    rel, ent = lax.axis_size("rel"), lax.axis_size("ent")
    low = 1 << ((ent.bit_length() - 1) // 2)
    high = ent // low
    per = relations // high
    here = lax.axis_index("rel")
    me = jnp.stack([lax.axis_index("ent"), here]).astype(jnp.int32)

    def near_swap(x, d):
        return swap(x, "ent", ent, d)

    def far_swap(x, d):
        return swap(x, "ent", ent, d * low)

    column = jnp.concatenate(from_partners(factors, high, lambda d: far_swap(factors, d)))
    nears = from_partners(column, low, lambda q: near_swap(column, q))[1:]

    half = rows // 2
    packed = observed[:, :half] | jnp.left_shift(observed[:, half:], 16)
    spare = -packed.shape[2] % LANES
    packed = jnp.pad(packed, ((0, 0), (0, 0), (0, spare)))

    def whole(shape):
        return pl.BlockSpec(shape, lambda t, me: (0,) * len(shape))

    def facts_block(first, s):
        return pl.BlockSpec(
            (relations, rows, rows),
            lambda t, me: (0, 0, chip_of(me[0], 2 * (t + first) + s, low, high)),
        )

    stack, pairs, first = relations * rows, ent // 2, high // 2
    wide = 2 * rows
    shape = jax.ShapeDtypeStruct
    cost = lambda share: pl.CostEstimate(
        flops=int(4 * stack * n_all * rank * share),
        bytes_accessed=int(4 * stack * n_all * share),
        transcendentals=0,
    )
    err, left, part = pl.pallas_call(
        functools.partial(early_kernel, low, high),
        grid_spec=pltpu.PrefetchScalarGridSpec(
            num_scalar_prefetch=1,
            grid=(first,),
            in_specs=[
                whole(packed.shape),
                facts_block(0, 0),
                facts_block(0, 1),
                whole((rows, rank)),
                whole(cores.shape),
                pl.BlockSpec((wide, rank), lambda t, me: (t, 0)),
            ],
            out_specs=[
                pl.BlockSpec((1, stack, wide), lambda t, me: (t, 0, 0)),
                whole((stack, rank)),
                whole((stack, rank)),
            ],
        ),
        out_shape=[
            shape((pairs, stack, wide), BF16),
            shape((stack, rank), BF16),
            shape((stack, rank), F32),
        ],
        cost_estimate=cost(first / pairs),
        compiler_params=pltpu.CompilerParams(vmem_limit_bytes=16 * MIB),
        name="early_kernel",
    )(me, packed, facts, facts, factors, cores, column)

    err, *pulls = pl.pallas_call(
        functools.partial(late_kernel, low, high, first),
        grid_spec=pltpu.PrefetchScalarGridSpec(
            num_scalar_prefetch=1,
            grid=(pairs - first,),
            in_specs=[
                whole(packed.shape),
                facts_block(first, 0),
                facts_block(first, 1),
                whole((stack, rank)),
                whole((stack, rank)),
                pl.BlockSpec(memory_space=pl.ANY),
            ]
            + [whole(column.shape)] * (low - 1),
            out_specs=[pl.BlockSpec((1, stack, wide), lambda t, me: (t + first, 0, 0))]
            + [whole((per * rows, rank))] * high,
            scratch_shapes=[pltpu.VMEM((wide, rank), BF16), pltpu.VMEM((stack, rank), F32)],
        ),
        out_shape=[shape(err.shape, BF16)] + [shape((per * rows, rank), BF16)] * high,
        input_output_aliases={6: 0},
        cost_estimate=cost(1 - first / pairs),
        compiler_params=pltpu.CompilerParams(vmem_limit_bytes=16 * MIB),
        name="late_kernel",
    )(me, packed, facts, facts, left, part, err, *nears)

    pulls = from_partners(pulls[0], high, lambda d: far_swap(pulls[d], d))

    sub = rows // rel
    rows_call = pl.pallas_call(
        functools.partial(rows_kernel, low, rel),
        grid_spec=pltpu.PrefetchScalarGridSpec(
            num_scalar_prefetch=1,
            grid=(pairs,),
            in_specs=[
                pl.BlockSpec((1, stack, wide), lambda t, me: ((t + 1) % pairs, 0, 0)),
                whole((stack, rank)),
                whole((relations * rank, rank)),
            ]
            + [whole(column.shape)] * low,
            out_specs=[whole((ent * sub, rank))] * rel,
            scratch_shapes=[
                pltpu.VMEM((wide, rank), BF16),
                pltpu.VMEM((wide, relations * rank), BF16),
                pltpu.VMEM((wide, rank), F32),
                pltpu.VMEM((rows, rank), F32),
            ],
        ),
        out_shape=[shape((ent * sub, rank), F32)] * rel,
        cost_estimate=cost(1.5),
        compiler_params=pltpu.CompilerParams(vmem_limit_bytes=16 * MIB),
        name="rows_kernel",
    )
    shares = rows_call(me, err, left, cores.reshape(relations * rank, rank), column, *nears)
    shares = [shares[0]] + [swap(shares[h], "rel", rel, h) for h in range(1, rel)]

    size = per * rank // low
    merged = pl.pallas_call(
        functools.partial(merge_kernel, low, high, rel),
        in_specs=[pl.BlockSpec(memory_space=pltpu.SMEM)]
        + [pl.BlockSpec(memory_space=pltpu.VMEM)] * (1 + high + rel),
        out_shape=[shape((high * sub + size, rank), F32)]
        + [shape((high * sub + size + scale_rows(high + 1), rank), I16)] * (low - 1),
        scratch_shapes=[pltpu.VMEM((per * rank, rank), F32)],
        compiler_params=pltpu.CompilerParams(vmem_limit_bytes=8 * MIB),
        name="merge_kernel",
    )(me, column, *pulls, *shares)
    merged = from_partners(merged[0], low, lambda q: near_swap(merged[q], q))

    mine, core_codes, *parts = pl.pallas_call(
        functools.partial(near_kernel, low, high, rank / n_all),
        out_shape=[shape((sub, rank), F32), shape((size + scale_rows(2), rank), I16)]
        + [shape((sub + size + scale_rows(2), rank), I16)] * (high - 1),
        compiler_params=pltpu.CompilerParams(vmem_limit_bytes=6 * MIB),
        name="near_kernel",
    )(*merged)
    parts = from_partners(None, high, lambda d: far_swap(parts[d - 1], d))[1:]

    owned, core_column = pl.pallas_call(
        functools.partial(far_kernel, low, high, n_all * relations * rel),
        in_specs=[pl.BlockSpec(memory_space=pltpu.SMEM)]
        + [pl.BlockSpec(memory_space=pltpu.VMEM)] * (high + 1),
        out_shape=[shape((sub, rank), F32), shape((high * size + scale_rows(high), rank), I16)],
        compiler_params=pltpu.CompilerParams(vmem_limit_bytes=4 * MIB),
        name="far_kernel",
    )(me, mine, core_codes, *parts)

    grad_factors = jnp.zeros((rel, sub, rank), F32)
    for h in range(rel):
        piece = owned if h == 0 else swap(owned, "rel", rel, h)
        grad_factors = lax.dynamic_update_index_in_dim(grad_factors, piece, here ^ h, 0)
    grad_factors = grad_factors.reshape(rows, rank)

    columns = from_partners(core_column, low, lambda q: near_swap(core_column, q))
    grad_cores = pl.pallas_call(
        functools.partial(place_kernel, low, high),
        in_specs=[pl.BlockSpec(memory_space=pltpu.SMEM)]
        + [pl.BlockSpec(memory_space=pltpu.VMEM)] * low,
        out_shape=shape((relations * rank, rank), F32),
        compiler_params=pltpu.CompilerParams(vmem_limit_bytes=4 * MIB),
        name="place_kernel",
    )(me, *columns)
    return grad_factors, grad_cores.reshape(relations, rank, rank)


def solution(mesh):
    return jax.shard_map(
        gradients,
        mesh=mesh,
        in_specs=(
            P("rel", "ent", None),
            P("rel", "ent", None),
            P("ent", None),
            P("rel", None, None),
        ),
        out_specs=(P("ent", None), P("rel", None, None)),
        check_vma=False,
    )
```

```python
import functools

import jax
import jax.numpy as jnp
from jax import lax
from jax.experimental import pallas as pl
from jax.experimental.pallas import tpu as pltpu
from jax.sharding import PartitionSpec as P


BITS = 13
STEPS = 128
TOP = 32700.0
LANES = 128
F32 = jnp.float32
BF16 = jnp.bfloat16
I16 = jnp.int16
MIB = 1 << 20


def swap(x, axis, size, distance):
    return lax.ppermute(x, axis, [(i, i ^ distance) for i in range(size)])


def from_partners(own, size, send):
    got = [own]
    for d in range(1, size):
        got.append(send(d))
    return got


def nt(a, b):
    return lax.dot_general(a, b, (((1,), (1,)), ((), ())), preferred_element_type=F32)


def tn(a, b):
    return lax.dot_general(a, b, (((0,), (0,)), ((), ())), preferred_element_type=F32)


def nn(a, b):
    return jnp.dot(a, b, preferred_element_type=F32)


def chip_of(me, slot, low, high):
    return jnp.bitwise_xor(me, (slot % high) * low + slot // high)


def take_pair(pieces, pair, scratch, size):
    inside = pieces[0].shape[0] // size
    for p, piece in enumerate(pieces):
        for i in range(inside):

            @pl.when(pair == p * inside + i)
            def _():
                scratch[...] = piece[i * size : (i + 1) * size, :]


def add_err(pair, me, low, high, left_ref, piece, words_ref, facts, err_ref, acc_ref):
    relations, half = words_ref.shape[0], words_ref.shape[1]
    rows, width = 2 * half, piece.shape[0] // 2
    lane = lax.broadcasted_iota(jnp.int32, (half, LANES), 1)
    words, bits, blocks = [], [], []
    for s in range(2):
        chip = chip_of(me, 2 * pair + s, low, high)
        column = lax.rem(chip, BITS) * LANES + lane
        word = jnp.right_shift(column * 5042, 16)
        words.append(word)
        bits.append(jnp.left_shift(1, column - word * BITS))
        blocks.append(pl.multiple_of(lax.div(chip, BITS) * LANES, LANES))

    def at(k):
        return slice(k * rows, (k + 1) * rows)

    whole_model = nt(left_ref[...], piece)
    errs = []
    for k in range(relations):
        model = whole_model[at(k), :]
        tiles = []
        for s in range(2):
            marks = jnp.take_along_axis(
                words_ref[k, :, pl.ds(blocks[s], LANES)], words[s], axis=1
            )
            data = facts[s][k].astype(F32)
            diff = model[:, s * width : (s + 1) * width] - data
            top = jnp.where((marks & bits[s]) != 0, diff[:half], 0.0)
            low_bits = jnp.left_shift(bits[s], 16)
            bottom = jnp.where((marks & low_bits) != 0, diff[half:], 0.0)
            tiles.append(jnp.concatenate([top, bottom], axis=0).astype(BF16))
        err = jnp.concatenate(tiles, axis=1)
        err_ref[0, at(k), :] = err
        errs.append(err)
    acc_ref[...] += nn(jnp.concatenate(errs, axis=0), piece)


def early_kernel(
    low, high, me_ref, words_ref, facts0_ref, facts1_ref, own_ref, cores_ref, column_ref,
    err_ref, left_ref, acc_ref,
):
    pair = pl.program_id(0)
    rows = own_ref.shape[0]

    @pl.when(pair == 0)
    def _():
        acc_ref[...] = jnp.zeros_like(acc_ref)
        for k in range(cores_ref.shape[0]):
            left_ref[k * rows : (k + 1) * rows, :] = nn(own_ref[...], cores_ref[k]).astype(BF16)

    add_err(
        pair, me_ref[0], low, high, left_ref, column_ref[...], words_ref,
        (facts0_ref, facts1_ref), err_ref, acc_ref,
    )


def late_kernel(
    low, high, first, me_ref, words_ref, facts0_ref, facts1_ref, left_ref, part_ref, _, *rest
):
    pieces, (err_ref, *pulls) = rest[: low - 1], rest[low - 1 : -2]
    piece_ref, acc_ref = rest[-2:]
    step = pl.program_id(0)

    @pl.when(step == 0)
    def _():
        acc_ref[...] = part_ref[...]

    take_pair(pieces, step, piece_ref, piece_ref.shape[0])
    add_err(
        step + first, me_ref[0], low, high, left_ref, piece_ref[...], words_ref,
        (facts0_ref, facts1_ref), err_ref, acc_ref,
    )

    @pl.when(step == pl.num_programs(0) - 1)
    def _():
        size = pulls[0].shape[0]
        far = me_ref[0] // low
        for d in range(high):
            at = pl.multiple_of(jnp.bitwise_xor(far, d) * size, size)
            pulls[d][...] = acc_ref[pl.ds(at, size), :].astype(BF16)


def rows_kernel(low, rel, me_ref, err_ref, left_ref, cores_ref, *rest):
    pieces, outs = rest[:low], rest[low : low + rel]
    piece_ref, _, total_ref, own_ref = rest[low + rel :]
    mine = me_ref[1]
    step, pairs = pl.program_id(0), pl.num_programs(0)
    pair = lax.rem(step + 1, pairs)

    @pl.when(step == 0)
    def _():
        own_ref[...] = jnp.zeros_like(own_ref)

    take_pair(pieces, pair, piece_ref, piece_ref.shape[0])
    rank = left_ref.shape[1]
    rows = piece_ref.shape[0] // 2
    relations = cores_ref.shape[0] // rank
    own = own_ref[...]
    right_all = nt(piece_ref[...], cores_ref[...]).astype(BF16)
    total_ref[...] = tn(err_ref[0], left_ref[...])
    for p in range(relations):
        own = own + nn(
            err_ref[0, p * rows : (p + 1) * rows, :], right_all[:, p * rank : (p + 1) * rank]
        )
    own_ref[...] = own

    @pl.when(step == pairs - 1)
    def _():
        total_ref[:rows, :] += own_ref[...]

    sub = rows // rel
    for h in range(rel):
        piece = jnp.bitwise_xor(mine, h) * sub
        for s in range(2):
            src = pl.multiple_of(piece + s * rows, sub)
            dst = pl.multiple_of((2 * pair + s) * sub, sub)
            outs[h][pl.ds(dst, sub), :] = total_ref[pl.ds(src, sub), :]


def scale_code(block):
    most = jnp.max(jnp.abs(block), axis=0, keepdims=True)
    return jnp.ceil(jnp.log2(jnp.maximum(most, 1e-30)) * STEPS).astype(jnp.int32)


def encode(block, code):
    factor = jnp.exp2(code.astype(F32) * (-1.0 / STEPS)) * TOP
    return jnp.floor(block * factor + 0.5).astype(jnp.int32).astype(jnp.int16)


def decode(codes, code):
    factor = jnp.exp2(code.astype(F32) * (1.0 / STEPS)) * (1.0 / TOP)
    return codes.astype(jnp.int32).astype(F32) * factor


def stack_codes(rows_of):
    at = lax.broadcasted_iota(jnp.int32, (scale_rows(len(rows_of)), LANES), 0)
    tile = jnp.zeros(at.shape, jnp.int32)
    for place, row in rows_of:
        tile = jnp.where(at == place, jnp.broadcast_to(row, at.shape), tile)
    return tile.astype(jnp.int16)


def scale_rows(blocks):
    return pl.cdiv(blocks, 16) * 16


def merge_kernel(low, high, rel, me_ref, column_ref, *rest):
    pulls, shares, outs = rest[:high], rest[high : high + rel], rest[high + rel : -1]
    total_ref = rest[-1]
    rank = column_ref.shape[1]
    rows = column_ref.shape[0] // high
    near = jnp.bitwise_and(me_ref[0], low - 1)
    for k in range(pulls[0].shape[0] // rows):
        acc = tn(column_ref[:rows, :], pulls[0][k * rows : (k + 1) * rows, :])
        for d in range(1, high):
            acc = acc + tn(
                column_ref[d * rows : (d + 1) * rows, :], pulls[d][k * rows : (k + 1) * rows, :]
            )
        total_ref[k * rank : (k + 1) * rank, :] = acc
    size = total_ref.shape[0] // low
    sub = shares[0].shape[0] // low // high
    core_at = high * sub
    core_codes = []
    for b in range(low):
        block = total_ref[b * size : (b + 1) * size, :]
        core_codes.append(scale_code(block))
        coded = encode(block, core_codes[-1])
        for out in outs[1:]:
            out[core_at + b * size : core_at + (b + 1) * size, :] = coded
    for q in range(low):
        codes = []
        for d in range(high):
            at = slice((q * high + d) * sub, (q * high + d + 1) * sub)
            part = shares[0][at, :]
            for h in range(1, rel):
                part = part + shares[h][at, :]
            span = slice(d * sub, (d + 1) * sub)
            if q == 0:
                outs[q][span, :] = part
            else:
                codes.append(scale_code(part))
                outs[q][span, :] = encode(part, codes[-1])
        if q > 0:
            outs[q][core_at + low * size :, :] = stack_codes(list(enumerate(codes + core_codes)))


def near_kernel(low, high, scale, *rest):
    (own_ref, *parts), (owned_ref, *outs) = rest[: low + 1], rest[low + 1 :]
    sub, core_at = owned_ref.shape[0], own_ref.shape[0]
    size = (parts[0].shape[0] - core_at - scale_rows(high + low)) // low
    scales = [part[core_at + low * size :, :].astype(jnp.int32) for part in parts]
    sums = []
    for d in range(high):
        span = slice(d * sub, (d + 1) * sub)
        total = own_ref[span, :]
        for part, code in zip(parts[1:], scales[1:]):
            total = total + decode(part[span, :], code[d : d + 1, :])
        sums.append(total)
    owned_ref[...] = sums[0]
    core_codes = []
    for b in range(low):
        span = slice(core_at + b * size, core_at + (b + 1) * size)
        terms = [
            decode(part[span, :], code[high + b : high + b + 1, :])
            for part, code in zip(parts, scales)
        ]
        while len(terms) > 1:
            terms = [terms[i] + terms[i + 1] for i in range(0, len(terms), 2)]
        core = terms[0] * scale
        core_codes.append(scale_code(core))
        coded = encode(core, core_codes[-1])
        for out in outs:
            out[b * size : (b + 1) * size, :] = coded
    for d in range(1, high):
        code = scale_code(sums[d])
        out = outs[d - 1]
        out[low * size : low * size + sub, :] = encode(sums[d], code)
        out[low * size + sub :, :] = stack_codes(list(enumerate(core_codes + [code])))


def far_kernel(low, root, mine_ref, *rest):
    parts, owned_ref = rest[:-1], rest[-1]
    sub = owned_ref.shape[0]
    tile = scale_rows(low + 1)
    total = mine_ref[...]
    for part in parts:
        end = part.shape[0] - tile
        code = part[end:, :].astype(jnp.int32)
        total = total + decode(part[end - sub : end, :], code[low : low + 1, :])
    owned_ref[...] = total / jnp.sqrt(F32(root))


def place_kernel(low, high, size, me_ref, *rest):
    parts, (out_ref, block_ref, sems) = rest[:-3], rest[-3:]
    far = me_ref[0] // low
    copies = []
    for d in range(high):
        tile = parts[d].shape[0] - scale_rows(low + 1)
        code = parts[d][tile:, :].astype(jnp.int32)
        for b in range(low):
            span = slice(b * size, (b + 1) * size)
            block_ref[d, span, :] = decode(parts[d][span, :], code[b : b + 1, :])
        at = pl.multiple_of(jnp.bitwise_xor(far, d) * (low * size), low * size)
        copies.append(
            pltpu.make_async_copy(
                block_ref.at[d], out_ref.at[pl.ds(at, low * size), :], sems.at[d]
            )
        )
        copies[-1].start()
    for copy in copies:
        copy.wait()


def gradients(facts, observed, factors, cores):
    relations, rows, n_all = facts.shape
    rank = factors.shape[1]
    rel, ent = lax.axis_size("rel"), lax.axis_size("ent")
    low = 1 << ((ent.bit_length() - 1) // 2)
    high = ent // low
    per = relations // high
    here = lax.axis_index("rel")
    me = jnp.stack([lax.axis_index("ent"), here]).astype(jnp.int32)

    def near_swap(x, d):
        return swap(x, "ent", ent, d)

    def far_swap(x, d):
        return swap(x, "ent", ent, d * low)

    column = jnp.concatenate(from_partners(factors, high, lambda d: far_swap(factors, d)))
    nears = from_partners(column, low, lambda q: near_swap(column, q))[1:]

    half = rows // 2
    packed = observed[:, :half] | jnp.left_shift(observed[:, half:], 16)
    spare = -packed.shape[2] % LANES
    packed = jnp.pad(packed, ((0, 0), (0, 0), (0, spare)))

    def whole(shape):
        return pl.BlockSpec(shape, lambda t, me: (0,) * len(shape))

    def facts_block(first, s):
        return pl.BlockSpec(
            (relations, rows, rows),
            lambda t, me: (0, 0, chip_of(me[0], 2 * (t + first) + s, low, high)),
        )

    stack, pairs, first = relations * rows, ent // 2, high // 2
    wide = 2 * rows
    shape = jax.ShapeDtypeStruct
    cost = lambda share: pl.CostEstimate(
        flops=int(4 * stack * n_all * rank * share),
        bytes_accessed=int(4 * stack * n_all * share),
        transcendentals=0,
    )
    err, left, part = pl.pallas_call(
        functools.partial(early_kernel, low, high),
        grid_spec=pltpu.PrefetchScalarGridSpec(
            num_scalar_prefetch=1,
            grid=(first,),
            in_specs=[
                whole(packed.shape),
                facts_block(0, 0),
                facts_block(0, 1),
                whole((rows, rank)),
                whole(cores.shape),
                pl.BlockSpec((wide, rank), lambda t, me: (t, 0)),
            ],
            out_specs=[
                pl.BlockSpec((1, stack, wide), lambda t, me: (t, 0, 0)),
                whole((stack, rank)),
                whole((stack, rank)),
            ],
        ),
        out_shape=[
            shape((pairs, stack, wide), BF16),
            shape((stack, rank), BF16),
            shape((stack, rank), F32),
        ],
        cost_estimate=cost(first / pairs),
        compiler_params=pltpu.CompilerParams(vmem_limit_bytes=16 * MIB),
        name="early_kernel",
    )(me, packed, facts, facts, factors, cores, column)

    err, *pulls = pl.pallas_call(
        functools.partial(late_kernel, low, high, first),
        grid_spec=pltpu.PrefetchScalarGridSpec(
            num_scalar_prefetch=1,
            grid=(pairs - first,),
            in_specs=[
                whole(packed.shape),
                facts_block(first, 0),
                facts_block(first, 1),
                whole((stack, rank)),
                whole((stack, rank)),
                pl.BlockSpec(memory_space=pl.ANY),
            ]
            + [whole(column.shape)] * (low - 1),
            out_specs=[pl.BlockSpec((1, stack, wide), lambda t, me: (t + first, 0, 0))]
            + [whole((per * rows, rank))] * high,
            scratch_shapes=[pltpu.VMEM((wide, rank), BF16), pltpu.VMEM((stack, rank), F32)],
        ),
        out_shape=[shape(err.shape, BF16)] + [shape((per * rows, rank), BF16)] * high,
        input_output_aliases={6: 0},
        cost_estimate=cost(1 - first / pairs),
        compiler_params=pltpu.CompilerParams(vmem_limit_bytes=16 * MIB),
        name="late_kernel",
    )(me, packed, facts, facts, left, part, err, *nears)

    pulls = from_partners(pulls[0], high, lambda d: far_swap(pulls[d], d))

    sub = rows // rel
    rows_call = pl.pallas_call(
        functools.partial(rows_kernel, low, rel),
        grid_spec=pltpu.PrefetchScalarGridSpec(
            num_scalar_prefetch=1,
            grid=(pairs,),
            in_specs=[
                pl.BlockSpec((1, stack, wide), lambda t, me: ((t + 1) % pairs, 0, 0)),
                whole((stack, rank)),
                whole((relations * rank, rank)),
            ]
            + [whole(column.shape)] * low,
            out_specs=[whole((ent * sub, rank))] * rel,
            scratch_shapes=[
                pltpu.VMEM((wide, rank), BF16),
                pltpu.VMEM((wide, relations * rank), BF16),
                pltpu.VMEM((wide, rank), F32),
                pltpu.VMEM((rows, rank), F32),
            ],
        ),
        out_shape=[shape((ent * sub, rank), F32)] * rel,
        cost_estimate=cost(1.5),
        compiler_params=pltpu.CompilerParams(vmem_limit_bytes=16 * MIB),
        name="rows_kernel",
    )
    shares = rows_call(me, err, left, cores.reshape(relations * rank, rank), column, *nears)
    shares = [shares[0]] + [swap(shares[h], "rel", rel, h) for h in range(1, rel)]

    size = per * rank // low
    merged = pl.pallas_call(
        functools.partial(merge_kernel, low, high, rel),
        in_specs=[pl.BlockSpec(memory_space=pltpu.SMEM)]
        + [pl.BlockSpec(memory_space=pltpu.VMEM)] * (1 + high + rel),
        out_shape=[shape((high * sub, rank), F32)]
        + [shape((high * sub + low * size + scale_rows(high + low), rank), I16)] * (low - 1),
        scratch_shapes=[pltpu.VMEM((per * rank, rank), F32)],
        compiler_params=pltpu.CompilerParams(vmem_limit_bytes=8 * MIB),
        name="merge_kernel",
    )(me, column, *pulls, *shares)
    mine, sent = merged[:2]
    merged = from_partners(sent, low, lambda q: near_swap(merged[q], q))

    mine, *parts = pl.pallas_call(
        functools.partial(near_kernel, low, high, rank / n_all),
        out_shape=[shape((sub, rank), F32)]
        + [shape((low * size + sub + scale_rows(low + 1), rank), I16)] * (high - 1),
        compiler_params=pltpu.CompilerParams(vmem_limit_bytes=6 * MIB),
        name="near_kernel",
    )(mine, *merged)
    sent = parts[0]
    parts = from_partners(sent, high, lambda d: far_swap(parts[d - 1], d))

    owned = pl.pallas_call(
        functools.partial(far_kernel, low, n_all * relations * rel),
        out_shape=shape((sub, rank), F32),
        compiler_params=pltpu.CompilerParams(vmem_limit_bytes=4 * MIB),
        name="far_kernel",
    )(mine, *parts[1:])

    grad_factors = jnp.zeros((rel, sub, rank), F32)
    for h in range(rel):
        piece = owned if h == 0 else swap(owned, "rel", rel, h)
        grad_factors = lax.dynamic_update_index_in_dim(grad_factors, piece, here ^ h, 0)
    grad_factors = grad_factors.reshape(rows, rank)

    grad_cores = pl.pallas_call(
        functools.partial(place_kernel, low, high, size),
        in_specs=[pl.BlockSpec(memory_space=pltpu.SMEM)]
        + [pl.BlockSpec(memory_space=pltpu.VMEM)] * high,
        out_specs=pl.BlockSpec(memory_space=pl.ANY),
        out_shape=shape((relations * rank, rank), F32),
        scratch_shapes=[
            pltpu.VMEM((high, low * size, rank), F32),
            pltpu.SemaphoreType.DMA((high,)),
        ],
        compiler_params=pltpu.CompilerParams(vmem_limit_bytes=4 * MIB),
        name="place_kernel",
    )(me, *parts)
    return grad_factors, grad_cores.reshape(relations, rank, rank)


def solution(mesh):
    return jax.shard_map(
        gradients,
        mesh=mesh,
        in_specs=(
            P("rel", "ent", None),
            P("rel", "ent", None),
            P("ent", None),
            P("rel", None, None),
        ),
        out_specs=(P("ent", None), P("rel", None, None)),
        check_vma=False,
    )
```

```python
import functools

import jax
import jax.numpy as jnp
from jax import lax
from jax.experimental import pallas as pl
from jax.experimental.pallas import tpu as pltpu
from jax.sharding import PartitionSpec as P


BITS = 13
STEPS = 128
TOP = 32700.0
LANES = 128
F32 = jnp.float32
BF16 = jnp.bfloat16
I16 = jnp.int16
MIB = 1 << 20
LARGE = pltpu.CompilerParams(vmem_limit_bytes=24 * MIB)


def swap(x, axis, size, distance):
    return lax.ppermute(x, axis, [(i, i ^ distance) for i in range(size)])


def from_partners(own, size, send):
    got = [own]
    for d in range(1, size):
        got.append(send(d))
    return got


def nt(a, b):
    return lax.dot_general(a, b, (((1,), (1,)), ((), ())), preferred_element_type=F32)


def tn(a, b):
    return lax.dot_general(a, b, (((0,), (0,)), ((), ())), preferred_element_type=F32)


def nn(a, b):
    return jnp.dot(a, b, preferred_element_type=F32)


def chip_of(me, slot, low, high):
    return jnp.bitwise_xor(me, (slot % high) * low + slot // high)


def add_err(pair, me, low, high, left_ref, piece, words_ref, facts_ref, err_ref, at_pair, acc):
    relations, half = words_ref.shape[0], words_ref.shape[1]
    rows, width = 2 * half, piece.shape[0] // 2
    lane = lax.broadcasted_iota(jnp.int32, (half, LANES), 1)
    words, bits, blocks, columns = [], [], [], []
    for s in range(2):
        chip = chip_of(me, 2 * pair + s, low, high)
        column = lax.rem(chip, BITS) * LANES + lane
        word = jnp.right_shift(column * 5042, 16)
        words.append(word)
        bits.append(jnp.left_shift(1, column - word * BITS))
        blocks.append(pl.multiple_of(lax.div(chip, BITS) * LANES, LANES))
        columns.append(pl.multiple_of(chip * width, width))
    model = nt(left_ref[...], piece)
    errs = []
    for k in range(relations):
        at = slice(k * rows, (k + 1) * rows)
        tiles = []
        for s in range(2):
            marks = jnp.take_along_axis(
                words_ref[k, :, pl.ds(blocks[s], LANES)], words[s], axis=1
            )
            data = facts_ref[k, :, pl.ds(columns[s], width)].astype(F32)
            diff = model[at, s * width : (s + 1) * width] - data
            top = jnp.where((marks & bits[s]) != 0, diff[:half], 0.0)
            low_bits = jnp.left_shift(bits[s], 16)
            bottom = jnp.where((marks & low_bits) != 0, diff[half:], 0.0)
            tiles.append(jnp.concatenate([top, bottom], axis=0).astype(BF16))
        errs.append(jnp.concatenate(tiles, axis=1))
        err_ref[at_pair, at, :] = errs[-1]
    acc[...] += nn(jnp.concatenate(errs, axis=0), piece)


def early_kernel(
    low, high, me_ref, words_ref, facts_ref, own_ref, cores_ref, column_ref,
    err_ref, left_ref, acc_ref,
):
    rows = own_ref.shape[0]
    acc_ref[...] = jnp.zeros_like(acc_ref)
    for k in range(cores_ref.shape[0]):
        left_ref[k * rows : (k + 1) * rows, :] = nn(own_ref[...], cores_ref[k]).astype(BF16)
    for pair in range(err_ref.shape[0]):
        piece = column_ref[2 * pair * rows : 2 * (pair + 1) * rows, :]
        add_err(
            pair, me_ref[0], low, high, left_ref, piece, words_ref, facts_ref, err_ref, pair, acc_ref
        )


def late_kernel(low, high, me_ref, words_ref, facts_ref, left_ref, part_ref, *rest):
    pieces, (err_ref, *pulls) = rest[: low - 1], rest[low - 1 : -1]
    acc_ref = rest[-1]
    acc_ref[...] = part_ref[...]
    first = high // 2
    wide = err_ref.shape[2]
    for step in range(err_ref.shape[0]):
        q, inside = divmod(step, first)
        piece = pieces[q][inside * wide : (inside + 1) * wide, :]
        add_err(
            step + first, me_ref[0], low, high, left_ref, piece, words_ref, facts_ref,
            err_ref, step, acc_ref,
        )
    size = pulls[0].shape[0]
    far = me_ref[0] // low
    for d in range(high):
        at = pl.multiple_of(jnp.bitwise_xor(far, d) * size, size)
        pulls[d][...] = acc_ref[pl.ds(at, size), :].astype(BF16)


def rows_kernel(rel, me_ref, err_ref, left_ref, cores_ref, *rest):
    pieces, outs, total_ref = rest[: -rel - 1], rest[-rel - 1 : -1], rest[-1]
    mine = me_ref[1]
    rank = left_ref.shape[1]
    wide = err_ref.shape[2]
    rows = wide // 2
    sub = rows // rel
    relations = cores_ref.shape[0] // rank
    inside = pieces[0].shape[0] // wide
    own = None

    def put(block, at):
        for h in range(rel):
            src = pl.multiple_of(at + jnp.bitwise_xor(mine, h) * sub, sub)
            outs[h][block * sub : (block + 1) * sub, :] = total_ref[pl.ds(src, sub), :]

    pairs = err_ref.shape[0]
    for pair in range(pairs):
        q, at = divmod(pair, inside)
        piece = pieces[q][at * wide : (at + 1) * wide, :]
        right = nt(piece, cores_ref[...]).astype(BF16)
        start = pair * wide
        total_ref[start : start + wide, :] = tn(err_ref[pair], left_ref[...])
        for k in range(relations):
            term = nn(err_ref[pair, k * rows : (k + 1) * rows, :], right[:, k * rank : (k + 1) * rank])
            own = term if own is None else own + term
        for s in range(2):
            put(2 * pair + s, start + s * rows)
    total_ref[pairs * wide :, :] = own
    put(2 * pairs, pairs * wide)


def scale_code(block):
    most = jnp.max(jnp.abs(block), axis=0, keepdims=True)
    return jnp.ceil(jnp.log2(jnp.maximum(most, 1e-30)) * STEPS).astype(jnp.int32)


def encode(block, code):
    factor = jnp.exp2(code.astype(F32) * (-1.0 / STEPS)) * TOP
    return jnp.floor(block * factor + 0.5).astype(jnp.int32).astype(jnp.int16)


def decode(codes, code):
    factor = jnp.exp2(code.astype(F32) * (1.0 / STEPS)) * (1.0 / TOP)
    return codes.astype(jnp.int32).astype(F32) * factor


def stack_codes(rows_of):
    at = lax.broadcasted_iota(jnp.int32, (scale_rows(len(rows_of)), LANES), 0)
    tile = jnp.zeros(at.shape, jnp.int32)
    for place, row in rows_of:
        tile = jnp.where(at == place, jnp.broadcast_to(row, at.shape), tile)
    return tile.astype(jnp.int16)


def scale_rows(blocks):
    return pl.cdiv(blocks, 16) * 16


def merge_kernel(low, high, rel, me_ref, column_ref, *rest):
    pulls, early = rest[:high], rest[high : high + rel]
    late, outs, total_ref = rest[high + rel : high + 2 * rel], rest[high + 2 * rel : -1], rest[-1]
    rank = column_ref.shape[1]
    rows = column_ref.shape[0] // high
    near = jnp.bitwise_and(me_ref[0], low - 1)
    for k in range(pulls[0].shape[0] // rows):
        acc = tn(column_ref[:rows, :], pulls[0][k * rows : (k + 1) * rows, :])
        for d in range(1, high):
            acc = acc + tn(
                column_ref[d * rows : (d + 1) * rows, :], pulls[d][k * rows : (k + 1) * rows, :]
            )
        total_ref[k * rank : (k + 1) * rank, :] = acc
    size = total_ref.shape[0] // low
    sub = early[0].shape[0] // (high + 1)
    core_at = high * sub
    core_codes = []
    for b in range(low):
        block = total_ref[b * size : (b + 1) * size, :]
        core_codes.append(scale_code(block))
        coded = encode(block, core_codes[-1])
        for out in outs[1:]:
            out[core_at + b * size : core_at + (b + 1) * size, :] = coded
    for q in range(low):
        codes = []
        for d in range(high):
            shares, slot = (early, d) if q == 0 else (late, (q - 1) * high + d)
            part = shares[0][slot * sub : (slot + 1) * sub, :]
            for h in range(1, rel):
                part = part + shares[h][slot * sub : (slot + 1) * sub, :]
            if q == 0 and d == 0:
                for share in early + late:
                    part = part + share[share.shape[0] - sub :, :]
            span = slice(d * sub, (d + 1) * sub)
            if q == 0:
                outs[q][span, :] = part
            else:
                codes.append(scale_code(part))
                outs[q][span, :] = encode(part, codes[-1])
        if q > 0:
            outs[q][core_at + low * size :, :] = stack_codes(list(enumerate(codes + core_codes)))


def near_kernel(low, high, scale, *rest):
    (own_ref, *parts), (owned_ref, *outs) = rest[: low + 1], rest[low + 1 :]
    sub, core_at = owned_ref.shape[0], own_ref.shape[0]
    size = (parts[0].shape[0] - core_at - scale_rows(high + low)) // low
    scales = [part[core_at + low * size :, :].astype(jnp.int32) for part in parts]
    sums = []
    for d in range(high):
        span = slice(d * sub, (d + 1) * sub)
        total = own_ref[span, :]
        for part, code in zip(parts[1:], scales[1:]):
            total = total + decode(part[span, :], code[d : d + 1, :])
        sums.append(total)
    owned_ref[...] = sums[0]
    core_codes = []
    for b in range(low):
        span = slice(core_at + b * size, core_at + (b + 1) * size)
        terms = [
            decode(part[span, :], code[high + b : high + b + 1, :])
            for part, code in zip(parts, scales)
        ]
        while len(terms) > 1:
            terms = [terms[i] + terms[i + 1] for i in range(0, len(terms), 2)]
        core = terms[0] * scale
        core_codes.append(scale_code(core))
        coded = encode(core, core_codes[-1])
        for out in outs:
            out[b * size : (b + 1) * size, :] = coded
    for d in range(1, high):
        code = scale_code(sums[d])
        out = outs[d - 1]
        out[low * size : low * size + sub, :] = encode(sums[d], code)
        out[low * size + sub :, :] = stack_codes(list(enumerate(core_codes + [code])))


def far_kernel(low, root, mine_ref, *rest):
    parts, owned_ref = rest[:-1], rest[-1]
    sub = owned_ref.shape[0]
    tile = scale_rows(low + 1)
    total = mine_ref[...]
    for part in parts:
        end = part.shape[0] - tile
        code = part[end:, :].astype(jnp.int32)
        total = total + decode(part[end - sub : end, :], code[low : low + 1, :])
    owned_ref[...] = total / jnp.sqrt(F32(root))


def place_kernel(low, high, size, me_ref, *rest):
    parts, (out_ref, block_ref, sems) = rest[:-3], rest[-3:]
    far = me_ref[0] // low
    copies = []
    for d in range(high):
        tile = parts[d].shape[0] - scale_rows(low + 1)
        code = parts[d][tile:, :].astype(jnp.int32)
        for b in range(low):
            span = slice(b * size, (b + 1) * size)
            block_ref[d, span, :] = decode(parts[d][span, :], code[b : b + 1, :])
        at = pl.multiple_of(jnp.bitwise_xor(far, d) * (low * size), low * size)
        copies.append(
            pltpu.make_async_copy(
                block_ref.at[d], out_ref.at[pl.ds(at, low * size), :], sems.at[d]
            )
        )
        copies[-1].start()
    for copy in copies:
        copy.wait()


def gradients(facts, observed, factors, cores):
    relations, rows, n_all = facts.shape
    rank = factors.shape[1]
    rel, ent = lax.axis_size("rel"), lax.axis_size("ent")
    low = 1 << ((ent.bit_length() - 1) // 2)
    high = ent // low
    per = relations // high
    here = lax.axis_index("rel")
    me = jnp.stack([lax.axis_index("ent"), here]).astype(jnp.int32)

    def near_swap(x, d):
        return swap(x, "ent", ent, d)

    def far_swap(x, d):
        return swap(x, "ent", ent, d * low)

    column = jnp.concatenate(from_partners(factors, high, lambda d: far_swap(factors, d)))
    nears = from_partners(column, low, lambda q: near_swap(column, q))[1:]

    half = rows // 2
    packed = observed[:, :half] | jnp.left_shift(observed[:, half:], 16)
    spare = -packed.shape[2] % LANES
    packed = jnp.pad(packed, ((0, 0), (0, 0), (0, spare)))

    stack, pairs, first = relations * rows, ent // 2, high // 2
    wide = 2 * rows
    sub = rows // rel
    shape = jax.ShapeDtypeStruct
    smem = pl.BlockSpec(memory_space=pltpu.SMEM)
    vmem = pl.BlockSpec(memory_space=pltpu.VMEM)

    def cost(share):
        return pl.CostEstimate(
            flops=int(4 * stack * n_all * rank * share),
            bytes_accessed=int(4 * stack * n_all * share),
            transcendentals=0,
        )

    early_call = pl.pallas_call(
        functools.partial(early_kernel, low, high),
        in_specs=[smem] + [vmem] * 5,
        out_shape=[
            shape((first, stack, wide), BF16),
            shape((stack, rank), BF16),
            shape((stack, rank), F32),
        ],
        compiler_params=LARGE,
        cost_estimate=cost(first / pairs),
        name="early_kernel",
    )
    early_err, left, part = early_call(me, packed, facts, factors, cores, column)

    def rows_call(blocks):
        return pl.pallas_call(
            functools.partial(rows_kernel, rel),
            in_specs=[smem] + [vmem] * (3 + (1 if blocks == first else low - 1)),
            out_shape=[shape(((2 * blocks + 1) * sub, rank), F32)] * rel,
            scratch_shapes=[pltpu.VMEM((blocks * wide + rows, rank), F32)],
            compiler_params=LARGE,
            cost_estimate=cost(1.5 * blocks / pairs),
            name="rows_kernel",
        )

    stacked = cores.reshape(relations * rank, rank)
    early_shares = rows_call(first)(me, early_err, left, stacked, column)

    late_call = pl.pallas_call(
        functools.partial(late_kernel, low, high),
        in_specs=[smem] + [vmem] * (3 + low),
        out_shape=[shape((pairs - first, stack, wide), BF16)]
        + [shape((per * rows, rank), BF16)] * high,
        scratch_shapes=[pltpu.VMEM((stack, rank), F32)],
        compiler_params=LARGE,
        cost_estimate=cost(1 - first / pairs),
        name="late_kernel",
    )
    late_err, *pulls = late_call(me, packed, facts, left, part, *nears)
    pulls = from_partners(pulls[0], high, lambda d: far_swap(pulls[d], d))

    late_shares = rows_call(pairs - first)(me, late_err, left, stacked, *nears)
    early_shares = from_partners(early_shares[0], rel, lambda h: swap(early_shares[h], "rel", rel, h))
    late_shares = from_partners(late_shares[0], rel, lambda h: swap(late_shares[h], "rel", rel, h))

    size = per * rank // low
    merged = pl.pallas_call(
        functools.partial(merge_kernel, low, high, rel),
        in_specs=[pl.BlockSpec(memory_space=pltpu.SMEM)]
        + [pl.BlockSpec(memory_space=pltpu.VMEM)] * (1 + high + 2 * rel),
        out_shape=[shape((high * sub, rank), F32)]
        + [shape((high * sub + low * size + scale_rows(high + low), rank), I16)] * (low - 1),
        scratch_shapes=[pltpu.VMEM((per * rank, rank), F32)],
        compiler_params=pltpu.CompilerParams(vmem_limit_bytes=8 * MIB),
        name="merge_kernel",
    )(me, column, *pulls, *early_shares, *late_shares)
    mine, sent = merged[:2]
    merged = from_partners(sent, low, lambda q: near_swap(merged[q], q))

    mine, *parts = pl.pallas_call(
        functools.partial(near_kernel, low, high, rank / n_all),
        out_shape=[shape((sub, rank), F32)]
        + [shape((low * size + sub + scale_rows(low + 1), rank), I16)] * (high - 1),
        compiler_params=pltpu.CompilerParams(vmem_limit_bytes=6 * MIB),
        name="near_kernel",
    )(mine, *merged)
    sent = parts[0]
    parts = from_partners(sent, high, lambda d: far_swap(parts[d - 1], d))

    owned = pl.pallas_call(
        functools.partial(far_kernel, low, n_all * relations * rel),
        out_shape=shape((sub, rank), F32),
        compiler_params=pltpu.CompilerParams(vmem_limit_bytes=4 * MIB),
        name="far_kernel",
    )(mine, *parts[1:])

    grad_factors = jnp.zeros((rel, sub, rank), F32)
    for h in range(rel):
        piece = owned if h == 0 else swap(owned, "rel", rel, h)
        grad_factors = lax.dynamic_update_index_in_dim(grad_factors, piece, here ^ h, 0)
    grad_factors = grad_factors.reshape(rows, rank)

    grad_cores = pl.pallas_call(
        functools.partial(place_kernel, low, high, size),
        in_specs=[pl.BlockSpec(memory_space=pltpu.SMEM)]
        + [pl.BlockSpec(memory_space=pltpu.VMEM)] * high,
        out_specs=pl.BlockSpec(memory_space=pl.ANY),
        out_shape=shape((relations * rank, rank), F32),
        scratch_shapes=[
            pltpu.VMEM((high, low * size, rank), F32),
            pltpu.SemaphoreType.DMA((high,)),
        ],
        compiler_params=pltpu.CompilerParams(vmem_limit_bytes=4 * MIB),
        name="place_kernel",
    )(me, *parts)
    return grad_factors, grad_cores.reshape(relations, rank, rank)


def solution(mesh):
    return jax.shard_map(
        gradients,
        mesh=mesh,
        in_specs=(
            P("rel", "ent", None),
            P("rel", "ent", None),
            P("ent", None),
            P("rel", None, None),
        ),
        out_specs=(P("ent", None), P("rel", None, None)),
        check_vma=False,
    )
```

```python
import functools

import jax
import jax.numpy as jnp
from jax import lax
from jax.experimental import pallas as pl
from jax.experimental.pallas import tpu as pltpu
from jax.sharding import PartitionSpec as P


BITS = 13
STEPS = 128
TOP = 32700.0
LANES = 128
F32 = jnp.float32
BF16 = jnp.bfloat16
I16 = jnp.int16
MIB = 1 << 20
LARGE = pltpu.CompilerParams(vmem_limit_bytes=24 * MIB)


def swap(x, axis, size, distance):
    return lax.ppermute(x, axis, [(i, i ^ distance) for i in range(size)])


def from_partners(own, size, send):
    got = [own]
    for d in range(1, size):
        got.append(send(d))
    return got


def nt(a, b):
    return lax.dot_general(a, b, (((1,), (1,)), ((), ())), preferred_element_type=F32)


def tn(a, b):
    return lax.dot_general(a, b, (((0,), (0,)), ((), ())), preferred_element_type=F32)


def nn(a, b):
    return jnp.dot(a, b, preferred_element_type=F32)


def chip_of(me, slot, low, high):
    return jnp.bitwise_xor(me, (slot % high) * low + slot // high)


def add_err(pair, me, low, high, left_ref, piece, words_ref, facts_ref, err_ref, at_pair, acc):
    relations, half = words_ref.shape[0], words_ref.shape[1]
    rows, width = 2 * half, piece.shape[0] // 2
    lane = lax.broadcasted_iota(jnp.int32, (half, LANES), 1)
    words, bits, blocks, columns = [], [], [], []
    for s in range(2):
        chip = chip_of(me, 2 * pair + s, low, high)
        column = lax.rem(chip, BITS) * LANES + lane
        word = jnp.right_shift(column * 5042, 16)
        words.append(word)
        bits.append(jnp.left_shift(1, column - word * BITS))
        blocks.append(pl.multiple_of(lax.div(chip, BITS) * LANES, LANES))
        columns.append(pl.multiple_of(chip * width, width))
    model = nt(left_ref[...], piece)
    errs = []
    for k in range(relations):
        at = slice(k * rows, (k + 1) * rows)
        tiles = []
        for s in range(2):
            marks = jnp.take_along_axis(
                words_ref[k, :, pl.ds(blocks[s], LANES)], words[s], axis=1
            )
            data = facts_ref[k, :, pl.ds(columns[s], width)].astype(F32)
            diff = model[at, s * width : (s + 1) * width] - data
            top = jnp.where((marks & bits[s]) != 0, diff[:half], 0.0)
            low_bits = jnp.left_shift(bits[s], 16)
            bottom = jnp.where((marks & low_bits) != 0, diff[half:], 0.0)
            tiles.append(jnp.concatenate([top, bottom], axis=0).astype(BF16))
        errs.append(jnp.concatenate(tiles, axis=1))
        err_ref[at_pair, at, :] = errs[-1]
    acc[...] += nn(jnp.concatenate(errs, axis=0), piece)


def early_kernel(
    low, high, me_ref, words_ref, facts_ref, own_ref, cores_ref, column_ref,
    err_ref, left_ref, acc_ref,
):
    rows = own_ref.shape[0]
    acc_ref[...] = jnp.zeros_like(acc_ref)
    for k in range(cores_ref.shape[0]):
        left_ref[k * rows : (k + 1) * rows, :] = nn(own_ref[...], cores_ref[k]).astype(BF16)
    for pair in range(err_ref.shape[0]):
        piece = column_ref[2 * pair * rows : 2 * (pair + 1) * rows, :]
        add_err(
            pair, me_ref[0], low, high, left_ref, piece, words_ref, facts_ref, err_ref, pair, acc_ref
        )


def late_kernel(low, high, me_ref, words_ref, facts_ref, left_ref, part_ref, *rest):
    pieces, (err_ref, *pulls) = rest[: low - 1], rest[low - 1 : -1]
    acc_ref = rest[-1]
    acc_ref[...] = part_ref[...]
    first = high // 2
    wide = err_ref.shape[2]
    for step in range(err_ref.shape[0]):
        q, inside = divmod(step, first)
        piece = pieces[q][inside * wide : (inside + 1) * wide, :]
        add_err(
            step + first, me_ref[0], low, high, left_ref, piece, words_ref, facts_ref,
            err_ref, step, acc_ref,
        )
    size = pulls[0].shape[0]
    far = me_ref[0] // low
    for d in range(high):
        at = pl.multiple_of(jnp.bitwise_xor(far, d) * size, size)
        pulls[d][...] = acc_ref[pl.ds(at, size), :].astype(BF16)


def rows_kernel(rel, me_ref, err_ref, left_ref, cores_ref, *rest):
    pieces, outs, total_ref = rest[: -rel - 1], rest[-rel - 1 : -1], rest[-1]
    mine = me_ref[1]
    rank = left_ref.shape[1]
    wide = err_ref.shape[2]
    rows = wide // 2
    sub = rows // rel
    relations = cores_ref.shape[0] // rank
    inside = pieces[0].shape[0] // wide
    own = None

    def put(block, at):
        for h in range(rel):
            src = pl.multiple_of(at + jnp.bitwise_xor(mine, h) * sub, sub)
            outs[h][block * sub : (block + 1) * sub, :] = total_ref[pl.ds(src, sub), :]

    pairs = len(pieces) * inside
    for pair in range(pairs):
        q, at = divmod(pair, inside)
        piece = pieces[q][at * wide : (at + 1) * wide, :]
        right = nt(piece, cores_ref[...]).astype(BF16)
        start = pair * wide
        total_ref[start : start + wide, :] = tn(err_ref[pair], left_ref[...])
        for k in range(relations):
            term = nn(
                err_ref[pair, k * rows : (k + 1) * rows, :], right[:, k * rank : (k + 1) * rank]
            )
            own = term if own is None else own + term
        for s in range(2):
            put(2 * pair + s, start + s * rows)
    total_ref[pairs * wide :, :] = own
    put(2 * pairs, pairs * wide)


def scale_code(block):
    most = jnp.max(jnp.abs(block), axis=0, keepdims=True)
    return jnp.ceil(jnp.log2(jnp.maximum(most, 1e-30)) * STEPS).astype(jnp.int32)


def encode(block, code):
    factor = jnp.exp2(code.astype(F32) * (-1.0 / STEPS)) * TOP
    return jnp.floor(block * factor + 0.5).astype(jnp.int32).astype(jnp.int16)


def decode(codes, code):
    factor = jnp.exp2(code.astype(F32) * (1.0 / STEPS)) * (1.0 / TOP)
    return codes.astype(jnp.int32).astype(F32) * factor


def stack_codes(rows_of):
    at = lax.broadcasted_iota(jnp.int32, (scale_rows(len(rows_of)), LANES), 0)
    tile = jnp.zeros(at.shape, jnp.int32)
    for place, row in rows_of:
        tile = jnp.where(at == place, jnp.broadcast_to(row, at.shape), tile)
    return tile.astype(jnp.int16)


def scale_rows(blocks):
    return pl.cdiv(blocks, 16) * 16


def core_kernel(low, high, column_ref, *rest):
    pulls, out_ref = rest[:high], rest[high]
    rows = column_ref.shape[0] // high
    total = []
    for k in range(pulls[0].shape[0] // rows):
        acc = None
        for d in range(high):
            term = tn(
                column_ref[d * rows : (d + 1) * rows, :], pulls[d][k * rows : (k + 1) * rows, :]
            )
            acc = term if acc is None else acc + term
        total.append(acc)
    total = jnp.concatenate(total, axis=0)
    size = total.shape[0] // low
    codes = []
    for b in range(low):
        block = total[b * size : (b + 1) * size, :]
        codes.append(scale_code(block))
        out_ref[b * size : (b + 1) * size, :] = encode(block, codes[-1])
    out_ref[low * size :, :] = stack_codes(list(enumerate(codes)))


def merge_kernel(low, high, rel, core_ref, *rest):
    early, late, outs = rest[:rel], rest[rel : 2 * rel], rest[2 * rel :]
    sub = early[0].shape[0] // (high + 1)
    core_at = high * sub
    size = core_ref.shape[0] - scale_rows(low)
    core_codes = core_ref[size:, :].astype(jnp.int32)
    core_codes = [core_codes[b : b + 1, :] for b in range(low)]
    for q in range(low):
        codes = []
        for d in range(high):
            shares, slot = (early, d) if q == 0 else (late, (q - 1) * high + d)
            part = shares[0][slot * sub : (slot + 1) * sub, :]
            for h in range(1, rel):
                part = part + shares[h][slot * sub : (slot + 1) * sub, :]
            if q == 0 and d == 0:
                for share in early + late:
                    part = part + share[share.shape[0] - sub :, :]
            span = slice(d * sub, (d + 1) * sub)
            if q == 0:
                outs[q][span, :] = part
            else:
                codes.append(scale_code(part))
                outs[q][span, :] = encode(part, codes[-1])
        if q > 0:
            outs[q][core_at : core_at + size, :] = core_ref[:size, :]
            outs[q][core_at + size :, :] = stack_codes(list(enumerate(codes + core_codes)))


def near_kernel(low, high, scale, *rest):
    (own_ref, *parts), (owned_ref, *outs) = rest[: low + 1], rest[low + 1 :]
    sub, core_at = owned_ref.shape[0], own_ref.shape[0]
    size = (parts[0].shape[0] - core_at - scale_rows(high + low)) // low
    scales = [part[core_at + low * size :, :].astype(jnp.int32) for part in parts]
    sums = []
    for d in range(high):
        span = slice(d * sub, (d + 1) * sub)
        total = own_ref[span, :]
        for part, code in zip(parts[1:], scales[1:]):
            total = total + decode(part[span, :], code[d : d + 1, :])
        sums.append(total)
    owned_ref[...] = sums[0]
    core_codes = []
    for b in range(low):
        span = slice(core_at + b * size, core_at + (b + 1) * size)
        terms = [
            decode(part[span, :], code[high + b : high + b + 1, :])
            for part, code in zip(parts, scales)
        ]
        while len(terms) > 1:
            terms = [terms[i] + terms[i + 1] for i in range(0, len(terms), 2)]
        core = terms[0] * scale
        core_codes.append(scale_code(core))
        coded = encode(core, core_codes[-1])
        for out in outs:
            out[b * size : (b + 1) * size, :] = coded
    for d in range(1, high):
        code = scale_code(sums[d])
        out = outs[d - 1]
        out[low * size : low * size + sub, :] = encode(sums[d], code)
        out[low * size + sub :, :] = stack_codes(list(enumerate(core_codes + [code])))


def far_kernel(low, root, mine_ref, *rest):
    parts, owned_ref = rest[:-1], rest[-1]
    sub = owned_ref.shape[0]
    tile = scale_rows(low + 1)
    total = mine_ref[...]
    for part in parts:
        end = part.shape[0] - tile
        code = part[end:, :].astype(jnp.int32)
        total = total + decode(part[end - sub : end, :], code[low : low + 1, :])
    owned_ref[...] = total / jnp.sqrt(F32(root))


def place_kernel(low, high, size, me_ref, *rest):
    parts, (out_ref, block_ref, sems) = rest[:-3], rest[-3:]
    far = me_ref[0] // low
    copies = []
    for d in range(high):
        tile = parts[d].shape[0] - scale_rows(low + 1)
        code = parts[d][tile:, :].astype(jnp.int32)
        for b in range(low):
            span = slice(b * size, (b + 1) * size)
            block_ref[d, span, :] = decode(parts[d][span, :], code[b : b + 1, :])
        at = pl.multiple_of(jnp.bitwise_xor(far, d) * (low * size), low * size)
        copies.append(
            pltpu.make_async_copy(
                block_ref.at[d], out_ref.at[pl.ds(at, low * size), :], sems.at[d]
            )
        )
        copies[-1].start()
    for copy in copies:
        copy.wait()


def gradients(facts, observed, factors, cores):
    relations, rows, n_all = facts.shape
    rank = factors.shape[1]
    rel, ent = lax.axis_size("rel"), lax.axis_size("ent")
    low = 1 << ((ent.bit_length() - 1) // 2)
    high = ent // low
    per = relations // high
    here = lax.axis_index("rel")
    me = jnp.stack([lax.axis_index("ent"), here]).astype(jnp.int32)

    def near_swap(x, d):
        return swap(x, "ent", ent, d)

    def far_swap(x, d):
        return swap(x, "ent", ent, d * low)

    column = jnp.concatenate(from_partners(factors, high, lambda d: far_swap(factors, d)))
    nears = from_partners(column, low, lambda q: near_swap(column, q))[1:]

    half = rows // 2
    packed = observed[:, :half] | jnp.left_shift(observed[:, half:], 16)
    spare = -packed.shape[2] % LANES
    packed = jnp.pad(packed, ((0, 0), (0, 0), (0, spare)))

    stack, pairs, first = relations * rows, ent // 2, high // 2
    wide = 2 * rows
    sub = rows // rel
    shape = jax.ShapeDtypeStruct
    smem = pl.BlockSpec(memory_space=pltpu.SMEM)
    vmem = pl.BlockSpec(memory_space=pltpu.VMEM)

    def cost(share):
        return pl.CostEstimate(
            flops=int(4 * stack * n_all * rank * share),
            bytes_accessed=int(4 * stack * n_all * share),
            transcendentals=0,
        )

    early_call = pl.pallas_call(
        functools.partial(early_kernel, low, high),
        in_specs=[smem] + [vmem] * 5,
        out_shape=[
            shape((first, stack, wide), BF16),
            shape((stack, rank), BF16),
            shape((stack, rank), F32),
        ],
        compiler_params=LARGE,
        cost_estimate=cost(first / pairs),
        name="early_kernel",
    )
    early_err, left, part = early_call(me, packed, facts, factors, cores, column)

    def rows_call(blocks):
        return pl.pallas_call(
            functools.partial(rows_kernel, rel),
            in_specs=[smem] + [vmem] * (3 + blocks // first),
            out_shape=[shape(((2 * blocks + 1) * sub, rank), F32)] * rel,
            scratch_shapes=[pltpu.VMEM((blocks * wide + rows, rank), F32)],
            compiler_params=LARGE,
            cost_estimate=cost(1.5 * blocks / pairs),
            name="rows_kernel",
        )

    def halves(shares):
        return from_partners(shares[0], rel, lambda h: swap(shares[h], "rel", rel, h))

    stacked = cores.reshape(relations * rank, rank)
    early_shares = rows_call(first)(me, early_err, left, stacked, column)
    early_shares = halves(early_shares)

    late_call = pl.pallas_call(
        functools.partial(late_kernel, low, high),
        in_specs=[smem] + [vmem] * (3 + low),
        out_shape=[shape((pairs - first, stack, wide), BF16)]
        + [shape((per * rows, rank), BF16)] * high,
        scratch_shapes=[pltpu.VMEM((stack, rank), F32)],
        compiler_params=LARGE,
        cost_estimate=cost(1 - first / pairs),
        name="late_kernel",
    )
    late_err, *pulls = late_call(me, packed, facts, left, part, *nears)
    pulls = from_partners(pulls[0], high, lambda d: far_swap(pulls[d], d))

    late_shares = rows_call(pairs - first)(me, late_err, left, stacked, *nears)
    late_shares = halves(late_shares)

    size = per * rank // low
    core_call = pl.pallas_call(
        functools.partial(core_kernel, low, high),
        in_specs=[vmem] * (1 + high),
        out_shape=shape((low * size + scale_rows(low), rank), I16),
        compiler_params=pltpu.CompilerParams(vmem_limit_bytes=8 * MIB),
        cost_estimate=cost(0.1),
        name="core_kernel",
    )
    core_codes = core_call(column, *pulls)
    merged = pl.pallas_call(
        functools.partial(merge_kernel, low, high, rel),
        in_specs=[vmem] * (1 + 2 * rel),
        out_shape=[shape((high * sub, rank), F32)]
        + [shape((high * sub + low * size + scale_rows(high + low), rank), I16)] * (low - 1),
        compiler_params=pltpu.CompilerParams(vmem_limit_bytes=8 * MIB),
        name="merge_kernel",
    )(core_codes, *early_shares, *late_shares)
    mine, sent = merged[:2]
    merged = from_partners(sent, low, lambda q: near_swap(merged[q], q))

    mine, *parts = pl.pallas_call(
        functools.partial(near_kernel, low, high, rank / n_all),
        out_shape=[shape((sub, rank), F32)]
        + [shape((low * size + sub + scale_rows(low + 1), rank), I16)] * (high - 1),
        compiler_params=pltpu.CompilerParams(vmem_limit_bytes=6 * MIB),
        name="near_kernel",
    )(mine, *merged)
    sent = parts[0]
    parts = from_partners(sent, high, lambda d: far_swap(parts[d - 1], d))

    owned = pl.pallas_call(
        functools.partial(far_kernel, low, n_all * relations * rel),
        out_shape=shape((sub, rank), F32),
        compiler_params=pltpu.CompilerParams(vmem_limit_bytes=4 * MIB),
        name="far_kernel",
    )(mine, *parts[1:])

    grad_factors = jnp.zeros((rel, sub, rank), F32)
    for h in range(rel):
        piece = owned if h == 0 else swap(owned, "rel", rel, h)
        grad_factors = lax.dynamic_update_index_in_dim(grad_factors, piece, here ^ h, 0)
    grad_factors = grad_factors.reshape(rows, rank)

    grad_cores = pl.pallas_call(
        functools.partial(place_kernel, low, high, size),
        in_specs=[pl.BlockSpec(memory_space=pltpu.SMEM)]
        + [pl.BlockSpec(memory_space=pltpu.VMEM)] * high,
        out_specs=pl.BlockSpec(memory_space=pl.ANY),
        out_shape=shape((relations * rank, rank), F32),
        scratch_shapes=[
            pltpu.VMEM((high, low * size, rank), F32),
            pltpu.SemaphoreType.DMA((high,)),
        ],
        compiler_params=pltpu.CompilerParams(vmem_limit_bytes=4 * MIB),
        name="place_kernel",
    )(me, *parts)
    return grad_factors, grad_cores.reshape(relations, rank, rank)


def solution(mesh):
    return jax.shard_map(
        gradients,
        mesh=mesh,
        in_specs=(
            P("rel", "ent", None),
            P("rel", "ent", None),
            P("ent", None),
            P("rel", None, None),
        ),
        out_specs=(P("ent", None), P("rel", None, None)),
        check_vma=False,
    )
```

```python
import functools

import jax
import jax.numpy as jnp
from jax import lax
from jax.experimental import pallas as pl
from jax.experimental.pallas import tpu as pltpu
from jax.sharding import PartitionSpec as P


BITS = 13
STEPS = 128
TOP = 32700.0
LANES = 128
F32 = jnp.float32
BF16 = jnp.bfloat16
I16 = jnp.int16
MIB = 1 << 20
LARGE = pltpu.CompilerParams(vmem_limit_bytes=24 * MIB)


def swap(x, axis, size, distance):
    return lax.ppermute(x, axis, [(i, i ^ distance) for i in range(size)])


def from_partners(own, size, send):
    got = [own]
    for d in range(1, size):
        got.append(send(d))
    return got


def nt(a, b):
    return lax.dot_general(a, b, (((1,), (1,)), ((), ())), preferred_element_type=F32)


def tn(a, b):
    return lax.dot_general(a, b, (((0,), (0,)), ((), ())), preferred_element_type=F32)


def nn(a, b):
    return jnp.dot(a, b, preferred_element_type=F32)


def chip_of(me, slot, low, high):
    return jnp.bitwise_xor(me, (slot % high) * low + slot // high)


def add_err(pair, me, low, high, left_ref, piece, words_ref, facts_ref, err_ref, at_pair, acc):
    relations, half = words_ref.shape[0], words_ref.shape[1]
    rows, width = 2 * half, piece.shape[0] // 2
    lane = lax.broadcasted_iota(jnp.int32, (half, LANES), 1)
    words, bits, blocks, columns = [], [], [], []
    for s in range(2):
        chip = chip_of(me, 2 * pair + s, low, high)
        column = lax.rem(chip, BITS) * LANES + lane
        word = jnp.right_shift(column * 5042, 16)
        words.append(word)
        bits.append(jnp.left_shift(1, column - word * BITS))
        blocks.append(pl.multiple_of(lax.div(chip, BITS) * LANES, LANES))
        columns.append(pl.multiple_of(chip * width, width))
    model = nt(left_ref[...], piece)
    errs = []
    for k in range(relations):
        at = slice(k * rows, (k + 1) * rows)
        tiles = []
        for s in range(2):
            marks = jnp.take_along_axis(
                words_ref[k, :, pl.ds(blocks[s], LANES)], words[s], axis=1
            )
            data = facts_ref[k, :, pl.ds(columns[s], width)].astype(F32)
            diff = model[at, s * width : (s + 1) * width] - data
            top = jnp.where((marks & bits[s]) != 0, diff[:half], 0.0)
            low_bits = jnp.left_shift(bits[s], 16)
            bottom = jnp.where((marks & low_bits) != 0, diff[half:], 0.0)
            tiles.append(jnp.concatenate([top, bottom], axis=0).astype(BF16))
        errs.append(jnp.concatenate(tiles, axis=1))
        err_ref[at_pair, at, :] = errs[-1]
    acc[...] += nn(jnp.concatenate(errs, axis=0), piece)


def early_kernel(
    low, high, me_ref, words_ref, facts_ref, own_ref, cores_ref, column_ref,
    err_ref, left_ref, acc_ref,
):
    rows = own_ref.shape[0]
    acc_ref[...] = jnp.zeros_like(acc_ref)
    for k in range(cores_ref.shape[0]):
        left_ref[k * rows : (k + 1) * rows, :] = nn(own_ref[...], cores_ref[k]).astype(BF16)
    for pair in range(err_ref.shape[0]):
        piece = column_ref[2 * pair * rows : 2 * (pair + 1) * rows, :]
        add_err(
            pair, me_ref[0], low, high, left_ref, piece, words_ref, facts_ref, err_ref, pair, acc_ref
        )


def late_kernel(low, high, me_ref, words_ref, facts_ref, left_ref, part_ref, *rest):
    pieces, (err_ref, *pulls) = rest[: low - 1], rest[low - 1 : -1]
    acc_ref = rest[-1]
    acc_ref[...] = part_ref[...]
    first = high // 2
    wide = err_ref.shape[2]
    for step in range(err_ref.shape[0]):
        q, inside = divmod(step, first)
        piece = pieces[q][inside * wide : (inside + 1) * wide, :]
        add_err(
            step + first, me_ref[0], low, high, left_ref, piece, words_ref, facts_ref,
            err_ref, step, acc_ref,
        )
    size = pulls[0].shape[0]
    far = me_ref[0] // low
    for d in range(high):
        at = pl.multiple_of(jnp.bitwise_xor(far, d) * size, size)
        pulls[d][...] = acc_ref[pl.ds(at, size), :].astype(BF16)


def rows_kernel(rel, me_ref, err_ref, left_ref, cores_ref, *rest):
    pieces, outs, total_ref = rest[: -rel - 1], rest[-rel - 1 : -1], rest[-1]
    mine = me_ref[1]
    rank = left_ref.shape[1]
    wide = err_ref.shape[2]
    rows = wide // 2
    sub = rows // rel
    relations = cores_ref.shape[0] // rank
    inside = pieces[0].shape[0] // wide
    own = None

    def put(block, at):
        for h in range(rel):
            src = pl.multiple_of(at + jnp.bitwise_xor(mine, h) * sub, sub)
            outs[h][block * sub : (block + 1) * sub, :] = total_ref[pl.ds(src, sub), :]

    pairs = len(pieces) * inside
    for pair in range(pairs):
        q, at = divmod(pair, inside)
        piece = pieces[q][at * wide : (at + 1) * wide, :]
        right = nt(piece, cores_ref[...]).astype(BF16)
        start = pair * wide
        total_ref[start : start + wide, :] = tn(err_ref[pair], left_ref[...])
        for k in range(relations):
            term = nn(
                err_ref[pair, k * rows : (k + 1) * rows, :], right[:, k * rank : (k + 1) * rank]
            )
            own = term if own is None else own + term
        for s in range(2):
            put(2 * pair + s, start + s * rows)
    total_ref[pairs * wide :, :] = own
    put(2 * pairs, pairs * wide)


def scale_code(block):
    most = jnp.max(jnp.abs(block), axis=0, keepdims=True)
    return jnp.ceil(jnp.log2(jnp.maximum(most, 1e-30)) * STEPS).astype(jnp.int32)


def encode(block, code):
    factor = jnp.exp2(code.astype(F32) * (-1.0 / STEPS)) * TOP
    return jnp.floor(block * factor + 0.5).astype(jnp.int32).astype(jnp.int16)


def decode(codes, code):
    factor = jnp.exp2(code.astype(F32) * (1.0 / STEPS)) * (1.0 / TOP)
    return codes.astype(jnp.int32).astype(F32) * factor


def stack_codes(rows_of):
    at = lax.broadcasted_iota(jnp.int32, (scale_rows(len(rows_of)), LANES), 0)
    tile = jnp.zeros(at.shape, jnp.int32)
    for place, row in rows_of:
        tile = jnp.where(at == place, jnp.broadcast_to(row, at.shape), tile)
    return tile.astype(jnp.int16)


def scale_rows(blocks):
    return pl.cdiv(blocks, 16) * 16


def core_kernel(low, high, column_ref, *rest):
    pulls, out_ref = rest[:high], rest[high]
    rows = column_ref.shape[0] // high
    total = []
    for k in range(pulls[0].shape[0] // rows):
        acc = None
        for d in range(high):
            term = tn(
                column_ref[d * rows : (d + 1) * rows, :], pulls[d][k * rows : (k + 1) * rows, :]
            )
            acc = term if acc is None else acc + term
        total.append(acc)
    total = jnp.concatenate(total, axis=0)
    size = total.shape[0] // low
    codes = []
    for b in range(low):
        block = total[b * size : (b + 1) * size, :]
        codes.append(scale_code(block))
        out_ref[b * size : (b + 1) * size, :] = encode(block, codes[-1])
    out_ref[low * size :, :] = stack_codes(list(enumerate(codes)))


def merge_kernel(low, high, rel, core_ref, *rest):
    early, late, outs = rest[:rel], rest[rel : 2 * rel], rest[2 * rel :]
    sub = early[0].shape[0] // (high + 1)
    core_at = high * sub
    size = core_ref.shape[0] - scale_rows(low)
    core_codes = core_ref[size:, :].astype(jnp.int32)
    core_codes = [core_codes[b : b + 1, :] for b in range(low)]
    for q in range(low):
        codes = []
        for d in range(high):
            shares, slot = (early, d) if q == 0 else (late, (q - 1) * high + d)
            part = shares[0][slot * sub : (slot + 1) * sub, :]
            for h in range(1, rel):
                part = part + shares[h][slot * sub : (slot + 1) * sub, :]
            if q == 0 and d == 0:
                for share in early + late:
                    part = part + share[share.shape[0] - sub :, :]
            span = slice(d * sub, (d + 1) * sub)
            if q == 0:
                outs[q][span, :] = part
            else:
                codes.append(scale_code(part))
                outs[q][span, :] = encode(part, codes[-1])
        if q > 0:
            outs[q][core_at : core_at + size, :] = core_ref[:size, :]
            outs[q][core_at + size :, :] = stack_codes(list(enumerate(codes + core_codes)))


def near_kernel(low, high, scale, *rest):
    (own_ref, *parts), (owned_ref, *outs) = rest[: low + 1], rest[low + 1 :]
    sub, core_at = owned_ref.shape[0], own_ref.shape[0]
    size = (parts[0].shape[0] - core_at - scale_rows(high + low)) // low
    scales = [part[core_at + low * size :, :].astype(jnp.int32) for part in parts]
    sums = []
    for d in range(high):
        span = slice(d * sub, (d + 1) * sub)
        total = own_ref[span, :]
        for part, code in zip(parts[1:], scales[1:]):
            total = total + decode(part[span, :], code[d : d + 1, :])
        sums.append(total)
    owned_ref[...] = sums[0]
    core_codes = []
    for b in range(low):
        span = slice(core_at + b * size, core_at + (b + 1) * size)
        terms = [
            decode(part[span, :], code[high + b : high + b + 1, :])
            for part, code in zip(parts, scales)
        ]
        while len(terms) > 1:
            terms = [terms[i] + terms[i + 1] for i in range(0, len(terms), 2)]
        core = terms[0] * scale
        core_codes.append(scale_code(core))
        coded = encode(core, core_codes[-1])
        for out in outs:
            out[b * size : (b + 1) * size, :] = coded
    for d in range(1, high):
        code = scale_code(sums[d])
        out = outs[d - 1]
        out[low * size : low * size + sub, :] = encode(sums[d], code)
        out[low * size + sub :, :] = stack_codes(list(enumerate(core_codes + [code])))


def far_kernel(low, root, mine_ref, *rest):
    parts, owned_ref = rest[:-1], rest[-1]
    sub = owned_ref.shape[0]
    tile = scale_rows(low + 1)
    total = mine_ref[...]
    for part in parts:
        end = part.shape[0] - tile
        code = part[end:, :].astype(jnp.int32)
        total = total + decode(part[end - sub : end, :], code[low : low + 1, :])
    owned_ref[...] = total / jnp.sqrt(F32(root))


def place_kernel(low, size, first, me_ref, *rest):
    parts, (out_ref, block_ref, sems) = rest[:-3], rest[-3:]
    if first > 0:
        parts = parts[1:]
    far = me_ref[0] // low
    copies = []
    for d, part in enumerate(parts):
        tile = part.shape[0] - scale_rows(low + 1)
        code = part[tile:, :].astype(jnp.int32)
        for b in range(low):
            span = slice(b * size, (b + 1) * size)
            block_ref[d, span, :] = decode(part[span, :], code[b : b + 1, :])
        at = pl.multiple_of(jnp.bitwise_xor(far, d + first) * (low * size), low * size)
        copies.append(
            pltpu.make_async_copy(
                block_ref.at[d], out_ref.at[pl.ds(at, low * size), :], sems.at[d]
            )
        )
        copies[-1].start()
    for copy in copies:
        copy.wait()


def gradients(facts, observed, factors, cores):
    relations, rows, n_all = facts.shape
    rank = factors.shape[1]
    rel, ent = lax.axis_size("rel"), lax.axis_size("ent")
    low = 1 << ((ent.bit_length() - 1) // 2)
    high = ent // low
    per = relations // high
    here = lax.axis_index("rel")
    me = jnp.stack([lax.axis_index("ent"), here]).astype(jnp.int32)

    def near_swap(x, d):
        return swap(x, "ent", ent, d)

    def far_swap(x, d):
        return swap(x, "ent", ent, d * low)

    column = jnp.concatenate(from_partners(factors, high, lambda d: far_swap(factors, d)))
    nears = from_partners(column, low, lambda q: near_swap(column, q))[1:]

    half = rows // 2
    packed = observed[:, :half] | jnp.left_shift(observed[:, half:], 16)
    spare = -packed.shape[2] % LANES
    packed = jnp.pad(packed, ((0, 0), (0, 0), (0, spare)))

    stack, pairs, first = relations * rows, ent // 2, high // 2
    wide = 2 * rows
    sub = rows // rel
    shape = jax.ShapeDtypeStruct
    smem = pl.BlockSpec(memory_space=pltpu.SMEM)
    vmem = pl.BlockSpec(memory_space=pltpu.VMEM)

    def cost(share):
        return pl.CostEstimate(
            flops=int(4 * stack * n_all * rank * share),
            bytes_accessed=int(4 * stack * n_all * share),
            transcendentals=0,
        )

    early_call = pl.pallas_call(
        functools.partial(early_kernel, low, high),
        in_specs=[smem] + [vmem] * 5,
        out_shape=[
            shape((first, stack, wide), BF16),
            shape((stack, rank), BF16),
            shape((stack, rank), F32),
        ],
        compiler_params=LARGE,
        cost_estimate=cost(first / pairs),
        name="early_kernel",
    )
    early_err, left, part = early_call(me, packed, facts, factors, cores, column)

    def rows_call(blocks):
        return pl.pallas_call(
            functools.partial(rows_kernel, rel),
            in_specs=[smem] + [vmem] * (3 + blocks // first),
            out_shape=[shape(((2 * blocks + 1) * sub, rank), F32)] * rel,
            scratch_shapes=[pltpu.VMEM((blocks * wide + rows, rank), F32)],
            compiler_params=LARGE,
            cost_estimate=cost(1.5 * blocks / pairs),
            name="rows_kernel",
        )

    def halves(shares):
        return from_partners(shares[0], rel, lambda h: swap(shares[h], "rel", rel, h))

    stacked = cores.reshape(relations * rank, rank)
    early_shares = rows_call(first)(me, early_err, left, stacked, column)
    early_shares = halves(early_shares)

    late_call = pl.pallas_call(
        functools.partial(late_kernel, low, high),
        in_specs=[smem] + [vmem] * (3 + low),
        out_shape=[shape((pairs - first, stack, wide), BF16)]
        + [shape((per * rows, rank), BF16)] * high,
        scratch_shapes=[pltpu.VMEM((stack, rank), F32)],
        compiler_params=LARGE,
        cost_estimate=cost(1 - first / pairs),
        name="late_kernel",
    )
    late_err, *pulls = late_call(me, packed, facts, left, part, *nears)
    pulls = from_partners(pulls[0], high, lambda d: far_swap(pulls[d], d))

    late_shares = rows_call(pairs - first)(me, late_err, left, stacked, *nears)
    late_shares = halves(late_shares)

    size = per * rank // low
    core_call = pl.pallas_call(
        functools.partial(core_kernel, low, high),
        in_specs=[vmem] * (1 + high),
        out_shape=shape((low * size + scale_rows(low), rank), I16),
        compiler_params=pltpu.CompilerParams(vmem_limit_bytes=8 * MIB),
        cost_estimate=cost(0.1),
        name="core_kernel",
    )
    core_codes = core_call(column, *pulls)
    merged = pl.pallas_call(
        functools.partial(merge_kernel, low, high, rel),
        in_specs=[vmem] * (1 + 2 * rel),
        out_shape=[shape((high * sub, rank), F32)]
        + [shape((high * sub + low * size + scale_rows(high + low), rank), I16)] * (low - 1),
        compiler_params=pltpu.CompilerParams(vmem_limit_bytes=8 * MIB),
        name="merge_kernel",
    )(core_codes, *early_shares, *late_shares)
    mine, sent = merged[:2]
    merged = from_partners(sent, low, lambda q: near_swap(merged[q], q))

    mine, *parts = pl.pallas_call(
        functools.partial(near_kernel, low, high, rank / n_all),
        out_shape=[shape((sub, rank), F32)]
        + [shape((low * size + sub + scale_rows(low + 1), rank), I16)] * (high - 1),
        compiler_params=pltpu.CompilerParams(vmem_limit_bytes=6 * MIB),
        name="near_kernel",
    )(mine, *merged)
    sent = parts[0]
    parts = from_partners(sent, high, lambda d: far_swap(parts[d - 1], d))

    owned = pl.pallas_call(
        functools.partial(far_kernel, low, n_all * relations * rel),
        out_shape=shape((sub, rank), F32),
        compiler_params=pltpu.CompilerParams(vmem_limit_bytes=4 * MIB),
        name="far_kernel",
    )(mine, *parts[1:])

    grad_factors = jnp.zeros((rel, sub, rank), F32)
    for h in range(rel):
        piece = owned if h == 0 else swap(owned, "rel", rel, h)
        grad_factors = lax.dynamic_update_index_in_dim(grad_factors, piece, here ^ h, 0)
    grad_factors = grad_factors.reshape(rows, rank)

    def place(start, blocks, out):
        return pl.pallas_call(
            functools.partial(place_kernel, low, size, start),
            in_specs=[pl.BlockSpec(memory_space=pltpu.SMEM)]
            + [pl.BlockSpec(memory_space=pl.ANY)] * len(out)
            + [pl.BlockSpec(memory_space=pltpu.VMEM)] * len(blocks),
            out_specs=pl.BlockSpec(memory_space=pl.ANY),
            out_shape=shape((relations * rank, rank), F32),
            scratch_shapes=[
                pltpu.VMEM((len(blocks), low * size, rank), F32),
                pltpu.SemaphoreType.DMA((len(blocks),)),
            ],
            input_output_aliases={1: 0} if out else {},
            compiler_params=pltpu.CompilerParams(vmem_limit_bytes=4 * MIB),
            name="place_kernel",
        )(me, *out, *blocks)

    grad_cores = place(0, parts[:1], [])
    grad_cores = place(1, parts[1:], [grad_cores])
    return grad_factors, grad_cores.reshape(relations, rank, rank)


def solution(mesh):
    return jax.shard_map(
        gradients,
        mesh=mesh,
        in_specs=(
            P("rel", "ent", None),
            P("rel", "ent", None),
            P("ent", None),
            P("rel", None, None),
        ),
        out_specs=(P("ent", None), P("rel", None, None)),
        check_vma=False,
    )
```
